512 devices in a mesh: tm: 256 (over y, x, z_lo, core), chan: 2 (over z_hi).
Axes of the slice: x: 4, y: 4, z: 16 (z_hi: 2, z_lo: 8; z = z_hi * 8 + z_lo), core: 2. Of those that a mesh axis runs over, the one named last changes fastest.
Arguments:
- signal: bfloat16 [131072, 256], P('tm', 'chan'), may hold values from -6 to 6
- skip_in: bfloat16 [131072, 256], P('tm', 'chan'), may hold values from -6 to 6
- tap_weight: bfloat16 [4, 2, 256, 512], replicated, may hold values from -0.25 to 0.25
- tap_bias: float32 [4, 512], replicated, may hold values from -3 to 3
- res_weight: bfloat16 [3, 256, 256], replicated, may hold values from -0.375 to 0.375
- skip_weight: bfloat16 [4, 256, 256], replicated, may hold values from -0.375 to 0.375
- head_w1: float32 [256, 256], replicated, may hold values from -0.375 to 0.375
- head_b1: float32 [256], replicated, may hold values from -3 to 3
- head_w2: float32 [256, 12], replicated, may hold values from -0.375 to 0.375
- head_second_bias: float32 [12], replicated, may hold values from -3 to 3
- event_bin: int32 [1024], P('tm'), may hold values from 0 to 15
- observed: int32 [1024], P('tm'), may hold values 0 or 1
- valid_len: int32 [1], replicated, may hold values from 130817 to 131072
Outputs:
- window_nll: float32 [1024], P(('tm', 'chan'))
- grad_input: bfloat16 [131072, 256], P('tm', 'chan')
The draws below stay inside these ranges and needn't reach their ends.
All inputs are finite; a program needn't handle non-finite values. No bound on the sum of `observed` on one device may be relied on, other than what follows from the above.
Results may differ from the reference program's by a relative error of at most 0.022.
Values may be sent and summed in bfloat16 or wider, within the bound.
No kernel may reach another device: no remote copies, remote signals or barrier semaphores. Data moves between devices by JAX's collectives and lax.ppermute only.
A program may use at most 64 MiB of HBM per device.

```python
import jax
import jax.numpy as jnp
from jax import lax

C = 256
HID = 256
MIX = 4
NBINS = 16
LAYERS = 4
WLEN = 128
TL = 512
TOTAL = 131072
FIRST_DILATION = 8192
WINDOWS = 1024


def place_ends(drawn, rng, low, top_value):
    longest = drawn.shape.index(max(drawn.shape))
    spots = []
    for shift in (0, 1):
        where = [jax.random.randint(jax.random.fold_in(rng, axis), (), 0, length) for axis, length in enumerate(drawn.shape)]
        where[longest] = (where[longest] + shift) % drawn.shape[longest]
        spots.append(tuple(where))
    return drawn.at[spots[0]].set(low).at[spots[1]].set(top_value)


def block_scale(key, shape, pieces, low, largest):
    loudness = 1.0
    for axis_at, parts in pieces:
        steps = jax.random.uniform(jax.random.fold_in(jax.random.fold_in(key, 6), axis_at), (parts,), jnp.float32, low / len(pieces), largest / len(pieces))
        loudness = loudness * jnp.repeat(jnp.exp(steps), shape[axis_at] // parts).reshape((-1,) + (1,) * (len(shape) - 1 - axis_at))
    return loudness


def bell_draw(own_key, dims, deviation, most, pieces=(), held_as=jnp.bfloat16):
    result = jax.random.normal(own_key, dims, jnp.float32) * deviation
    if len(pieces) > 0:
        result = block_scale(own_key, dims, pieces, -0.22, 0.18) * result
    return jnp.clip(result, min=-most, max=most).astype(held_as)


def setup_inputs(seed: int = 0) -> dict:
    arg_keys = jax.random.split(jax.random.key(seed), 14)
    return {
        "signal": bell_draw(arg_keys[0], (TOTAL, C), 1.0, 6.0, ((0, 256), (1, 2))),
        "skip_in": bell_draw(arg_keys[1], (TOTAL, C), 1.0, 6.0, ((0, 256), (1, 2))),
        "tap_weight": bell_draw(arg_keys[2], (LAYERS, 2, C, 2 * C), (2 * C) ** -0.5, 0.25),
        "tap_bias": bell_draw(arg_keys[3], (LAYERS, 2 * C), 0.5, 3.0, (), jnp.float32),
        "res_weight": bell_draw(arg_keys[4], (LAYERS - 1, C, C), C ** -0.5, 0.375),
        "skip_weight": bell_draw(arg_keys[5], (LAYERS, C, C), C ** -0.5, 0.375),
        "head_w1": bell_draw(arg_keys[6], (C, HID), C ** -0.5, 0.375, (), jnp.float32),
        "head_b1": bell_draw(arg_keys[7], (HID,), 0.5, 3.0, (), jnp.float32),
        "head_w2": bell_draw(arg_keys[8], (HID, 3 * MIX), HID ** -0.5, 0.375, (), jnp.float32),
        "head_second_bias": bell_draw(arg_keys[9], (3 * MIX,), 0.5, 3.0, (), jnp.float32),
        "event_bin": place_ends(jax.random.randint(arg_keys[10], (WINDOWS,), 0, NBINS), jax.random.fold_in(arg_keys[10], 1), 0, NBINS - 1).astype(jnp.int32),
        "observed": place_ends((jax.random.randint(arg_keys[11], (WINDOWS,), 0, 3) < 2).astype(jnp.int32), jax.random.fold_in(arg_keys[11], 1), 0, 1),
        "valid_len": jax.random.randint(arg_keys[12], (1,), TOTAL - TL // 2 + 1, TOTAL + 1).astype(jnp.int32),
    }


def gate_values(preact, half_width):
    filters = jnp.tanh(preact[:, :half_width])
    gates = jax.nn.sigmoid(preact[:, half_width:])
    return (filters * gates).astype(jnp.bfloat16)

def gate_grads(preact, grad_gated, half_width):
    filters = jnp.tanh(preact[:, :half_width])
    gates = jax.nn.sigmoid(preact[:, half_width:])
    grad_filter = grad_gated * gates * (1.0 - filters * filters)
    gate_gradient = grad_gated * filters * gates * (1.0 - gates)
    return jnp.concatenate([grad_filter, gate_gradient], axis=1).astype(jnp.bfloat16)

def silu_slope(values):
    sig = jax.nn.sigmoid(values)
    return sig * (1.0 + values * (1.0 - sig))

def pool_windows(activity, keep_mask, window_len):
    row_count, width = activity.shape
    sums = (activity * keep_mask[:, None]).reshape(row_count // window_len, window_len, width).sum(axis=1)
    counts = keep_mask.reshape(row_count // window_len, window_len).sum(axis=1)
    return sums / jnp.maximum(counts, 1.0)[:, None]

def window_loss(pooled, bins, flags, head_w1, head_b1, head_w2, head_second_bias):
    hidden = jax.nn.silu(jnp.dot(pooled, head_w1, precision=lax.Precision.HIGHEST) + head_b1)
    params = jnp.dot(hidden, head_w2, precision=lax.Precision.HIGHEST) + head_second_bias
    mixes = params.shape[1] // 3
    logits = 4.0 * jnp.tanh(params[:, :mixes])
    mixture_log_weight = logits - jnp.log(lax.optimization_barrier(jnp.sum(jnp.exp(logits), axis=1, keepdims=True)))
    log_scale = jnp.tanh(params[:, mixes:2 * mixes])
    log_shape = 0.5 * jnp.tanh(params[:, 2 * mixes:])
    shape_value = jnp.exp(log_shape)
    log_time = jnp.log((bins.astype(jnp.float32) + 1.0) / 8.0)[:, None]
    ratio = log_time - log_scale
    power = jnp.exp(shape_value * ratio)
    log_density = log_shape - log_scale + (shape_value - 1.0) * ratio - power
    component = jnp.where(flags[:, None] == 1, log_density, -power)
    return -jnp.log(lax.optimization_barrier(jnp.sum(jnp.exp(mixture_log_weight + component), axis=1)))

def head_grads(pooled, bins, flags, head_w1, head_b1, head_w2, head_second_bias):

    def loss_of(values):
        return window_loss(values, bins, flags, head_w1, head_b1, head_w2, head_second_bias)
    nll_values, pullback = jax.vjp(loss_of, pooled)
    return (nll_values, pullback(jnp.ones_like(nll_values))[0])

def spread_rows(grad_pool, window_len):
    window_total_count, width = grad_pool.shape
    return jnp.broadcast_to(grad_pool[:, None, :], (window_total_count, window_len, width)).reshape(window_total_count * window_len, width)

def reference(signal, skip_in, tap_weight, tap_bias, res_weight, skip_weight, head_w1, head_b1, head_w2, head_second_bias, event_bin, observed, valid_len):
    total = signal.shape[0]
    width = signal.shape[1]
    current = signal
    skip_sum = skip_in.astype(jnp.float32)
    preacts = []
    for layer_number in range(LAYERS):
        delay_span_length = FIRST_DILATION * 2 ** layer_number
        delayed = jnp.concatenate([jnp.zeros((delay_span_length, width), jnp.bfloat16), current[:total - delay_span_length]], axis=0)
        preact = jnp.dot(delayed, tap_weight[layer_number, 0], preferred_element_type=jnp.float32)
        preact = preact + jnp.dot(current, tap_weight[layer_number, 1], preferred_element_type=jnp.float32) + tap_bias[layer_number]
        gated = gate_values(preact, width)
        preacts.append(preact)
        if layer_number < LAYERS - 1:
            current = (current.astype(jnp.float32) + jnp.dot(gated, res_weight[layer_number], preferred_element_type=jnp.float32)).astype(jnp.bfloat16)
        skip_sum = skip_sum + jnp.dot(gated, skip_weight[layer_number], preferred_element_type=jnp.float32)
    keep_mask = (jnp.arange(total, dtype=jnp.int32) < valid_len[0]).astype(jnp.float32)
    pooled = pool_windows(jax.nn.silu(skip_sum), keep_mask, WLEN)
    nll_values, grad_pool = head_grads(pooled, event_bin, observed, head_w1, head_b1, head_w2, head_second_bias)
    grad_skip = (spread_rows(grad_pool, WLEN) * keep_mask[:, None] * silu_slope(skip_sum)).astype(jnp.bfloat16)
    grad_rows = None
    for layer_number in range(LAYERS - 1, -1, -1):
        delay_span_length = FIRST_DILATION * 2 ** layer_number
        grad_gated = jnp.dot(grad_skip, skip_weight[layer_number].T, preferred_element_type=jnp.float32)
        if grad_rows is not None:
            grad_gated = grad_gated + jnp.dot(grad_rows, res_weight[layer_number].T, preferred_element_type=jnp.float32)
        preactivation_gradient = gate_grads(preacts[layer_number], grad_gated, width)
        ahead = jnp.concatenate([preactivation_gradient[delay_span_length:], jnp.zeros((delay_span_length, 2 * width), jnp.bfloat16)], axis=0)
        summed = jnp.dot(preactivation_gradient, tap_weight[layer_number, 1].T, preferred_element_type=jnp.float32)
        summed = summed + jnp.dot(ahead, tap_weight[layer_number, 0].T, preferred_element_type=jnp.float32)
        if grad_rows is not None:
            summed = summed + grad_rows.astype(jnp.float32)
        grad_rows = summed.astype(jnp.bfloat16)
    return (nll_values, grad_rows)
```

```python
import jax
import jax.numpy as jnp
from jax import lax
from jax.experimental import pallas as pl
from jax.experimental.pallas import tpu as pltpu
from jax.sharding import Mesh
from jax.sharding import PartitionSpec as P

WLEN = 128
FIRST_DILATION = 8192
F32 = jnp.float32
BF16 = jnp.bfloat16
EXACT = lax.Precision.HIGHEST


def dot(a, b):
    return jnp.dot(a, b, preferred_element_type=F32)


def dot_t(a, b, precision=None):
    return lax.dot_general(
        a, b, (((1,), (1,)), ((), ())), preferred_element_type=F32, precision=precision
    )


def sigmoid(v):
    return 0.5 * jnp.tanh(0.5 * v) + 0.5


def row_keep(limit, base, blocks, chunk, width):
    rows = lax.broadcasted_iota(jnp.int32, (blocks * chunk, width), 0)
    position = (rows // chunk) * FIRST_DILATION + rows % chunk + base
    return position < limit


def forward_kernel(
    blocks,
    chunk,
    place_ref,
    bin_ref,
    seen_ref,
    both_ref,
    tap_ref,
    bias_ref,
    res_ref,
    skipw_ref,
    tanh_ref,
    gate_ref,
    skip_ref,
    pool_ref,
):
    layers = tap_ref.shape[0]
    part = both_ref.shape[2] // 2
    width = 2 * part
    rows = blocks * chunk
    limit, base, chan_at = place_ref[0], place_ref[1], place_ref[2]
    whole = both_ref[...].reshape(2, rows, 2 * part)
    current = jnp.concatenate([whole[0, :, :part], whole[1, :, :part]], axis=1)
    skip_sum = jnp.concatenate([whole[0, :, part:], whole[1, :, part:]], axis=1).astype(F32)
    for layer in range(layers):
        late = chunk * 2**layer
        delayed = jnp.concatenate(
            [jnp.zeros((late, width), BF16), current[: rows - late]], axis=0
        )
        preact = (
            dot(delayed, tap_ref[layer, 0])
            + dot(current, tap_ref[layer, 1])
            + bias_ref[layer : layer + 1, :]
        )
        filters = jnp.tanh(preact[:, :width])
        gates = sigmoid(preact[:, width:])
        tanh_ref[layer] = filters
        gate_ref[layer] = gates
        gated = (filters * gates).astype(BF16)
        if layer < layers - 1:
            current = (current.astype(F32) + dot(gated, res_ref[layer])).astype(BF16)
        skip_sum = skip_sum + dot(gated, skipw_ref[layer])
    skip_ref[...] = skip_sum
    keep = row_keep(limit, base, blocks, chunk, width)
    active = jnp.where(keep, skip_sum * sigmoid(skip_sum), 0.0)
    sums = active.reshape(blocks, chunk, width).sum(axis=1)
    first = 2 * chan_at
    line = lax.broadcasted_iota(jnp.int32, (8, width), 0)
    extra = jnp.where(
        line == 0,
        bin_ref[first].astype(F32),
        jnp.where(
            line == 1,
            bin_ref[first + 1].astype(F32),
            jnp.where(line == 2, seen_ref[first].astype(F32), seen_ref[first + 1].astype(F32)),
        ),
    )
    for other in range(blocks):
        pool_ref[other, :blocks, :] = sums
        pool_ref[other, blocks:, :] = extra


def mixture(params, log_time, seen, mixes):
    lanes = params.shape[1]
    lane = lax.broadcasted_iota(jnp.int32, params.shape, 1)
    valid = lane < mixes
    bend_logit = jnp.tanh(params)
    log_scale = jnp.tanh(pltpu.roll(params, lanes - mixes, 1))
    bend_shape = jnp.tanh(pltpu.roll(params, lanes - 2 * mixes, 1))
    logits = 4.0 * bend_logit
    raised = jnp.where(valid, jnp.exp(logits), 0.0)
    total = jnp.sum(raised, axis=1, keepdims=True)
    log_weight = logits - jnp.log(total)
    log_shape = 0.5 * bend_shape
    shape = jnp.exp(log_shape)
    ratio = log_time - log_scale
    power = jnp.exp(shape * ratio)
    density = log_shape - log_scale + (shape - 1.0) * ratio - power
    component = jnp.where(seen, density, -power)
    likely = jnp.where(valid, jnp.exp(log_weight + component), 0.0)
    mass = jnp.sum(likely, axis=1, keepdims=True)
    nll = -jnp.log(mass)
    owned = likely / mass
    to_logit = (raised / total - owned) * 4.0 * (1.0 - bend_logit * bend_logit)
    steep = power * shape
    to_scale = jnp.where(seen, steep - shape, steep)
    to_shape = jnp.where(seen, 1.0 + shape * ratio, 0.0) - steep * ratio
    to_scale = -owned * to_scale * (1.0 - log_scale * log_scale)
    to_shape = -owned * to_shape * 0.5 * (1.0 - bend_shape * bend_shape)
    zero = jnp.zeros_like(params)
    grad = (
        jnp.where(valid, to_logit, zero)
        + pltpu.roll(jnp.where(valid, to_scale, zero), mixes, 1)
        + pltpu.roll(jnp.where(valid, to_shape, zero), 2 * mixes, 1)
    )
    return nll, grad


def backward_kernel(
    blocks,
    chunk,
    place_ref,
    pool_ref,
    tanh_ref,
    gate_ref,
    skip_ref,
    tap_ref,
    res_ref,
    skipw_ref,
    head1_ref,
    headb1_ref,
    head2_ref,
    headb2_ref,
    nll_ref,
    grad_ref,
    pad_ref,
):
    layers = tap_ref.shape[0]
    width = skip_ref.shape[1]
    part = width // 2
    rows = blocks * chunk
    lanes = pad_ref.shape[1]
    outs = head2_ref.shape[1]
    limit, base, chan_at, block_at, shard_base = (place_ref[i] for i in range(5))
    half = blocks // 2
    received = pool_ref[...]
    sums = jnp.concatenate(
        [
            received[:half, :blocks, :].sum(axis=0),
            received[half:, :blocks, :].sum(axis=0),
        ],
        axis=0,
    )
    bins = jnp.concatenate([received[:, blocks, :lanes], received[:, blocks + 1, :lanes]], axis=0)
    seen = (
        jnp.concatenate(
            [received[:, blocks + 2, :lanes], received[:, blocks + 3, :lanes]], axis=0
        )
        == 1.0
    )
    log_time = jnp.log((bins + 1.0) / 8.0)
    window = lax.broadcasted_iota(jnp.int32, (2 * blocks, width), 0)
    start = (
        (window % blocks) * FIRST_DILATION
        + shard_base
        + (2 * chan_at + window // blocks) * WLEN
    )
    count = jnp.clip(limit - start, 1, WLEN).astype(F32)
    pooled = sums / count
    pad_ref[...] = jnp.zeros_like(pad_ref)
    pad_ref[:width, :outs] = head2_ref[...]
    pad_ref[width : width + 1, :outs] = headb2_ref[...]
    head2 = pad_ref[:width, :]
    inner = (
        jnp.dot(pooled, head1_ref[...], preferred_element_type=F32, precision=EXACT)
        + headb1_ref[...]
    )
    open_inner = sigmoid(inner)
    hidden = inner * open_inner
    params = (
        jnp.dot(hidden, head2, preferred_element_type=F32, precision=EXACT)
        + pad_ref[width : width + 1, :]
    )
    nll, to_params = mixture(params, log_time, seen, outs // 3)
    to_hidden = dot_t(to_params, head2, EXACT)
    to_inner = to_hidden * open_inner * (1.0 + inner * (1.0 - open_inner))
    to_pooled = dot_t(to_inner, head1_ref[...], EXACT)

    row = lax.broadcasted_iota(jnp.int32, (2 * blocks, 2), 0)
    col = lax.broadcasted_iota(jnp.int32, (2 * blocks, 2), 1)
    mine = row == col * blocks + block_at
    nll_ref[...] = jnp.sum(jnp.where(mine, nll, 0.0), axis=0, keepdims=True)

    own_pool = jnp.where(block_at < half, to_pooled[:blocks], to_pooled[blocks:])
    spread = jnp.broadcast_to(own_pool[:, None, :], (blocks, chunk, width)).reshape(rows, width)
    keep = row_keep(limit, base, blocks, chunk, width)
    skip_sum = skip_ref[...]
    sig = sigmoid(skip_sum)
    slope = sig * (1.0 + skip_sum * (1.0 - sig))
    grad_skip = jnp.where(keep, spread * slope, 0.0).astype(BF16)
    grad_rows = None
    for layer in range(layers - 1, -1, -1):
        early = chunk * 2**layer
        grad_gated = dot_t(grad_skip, skipw_ref[layer])
        if grad_rows is not None:
            grad_gated = grad_gated + dot_t(grad_rows, res_ref[layer])
        filters = tanh_ref[layer]
        gates = gate_ref[layer]
        through = grad_gated * gates
        to_filter = (through * (1.0 - filters * filters)).astype(BF16)
        to_gate = (through * filters * (1.0 - gates)).astype(BF16)
        preact_grad = jnp.concatenate([to_filter, to_gate], axis=1)
        ahead = jnp.concatenate(
            [preact_grad[early:], jnp.zeros((early, 2 * width), BF16)], axis=0
        )
        summed = dot_t(preact_grad, tap_ref[layer, 1]) + dot_t(ahead, tap_ref[layer, 0])
        if grad_rows is not None:
            summed = summed + grad_rows.astype(F32)
        grad_rows = summed.astype(BF16)
    grad_ref[0] = grad_rows[:, :part].reshape(blocks, chunk, part)
    grad_ref[1] = grad_rows[:, part:].reshape(blocks, chunk, part)


def local(
    signal,
    skip_in,
    tap_weight,
    tap_bias,
    res_weight,
    skip_weight,
    head_w1,
    head_b1,
    head_w2,
    head_second_bias,
    event_bin,
    observed,
    valid_len,
):
    blocks = lax.axis_size("blk")
    chans = lax.axis_size("chan")
    shard_rows, part = signal.shape
    width = part * chans
    peers = blocks * chans
    chunk = shard_rows // peers
    rows = blocks * chunk
    layers = tap_weight.shape[0]
    block_at = lax.axis_index("blk")
    chan_at = lax.axis_index("chan")
    shard_base = lax.axis_index("j") * shard_rows
    base = shard_base + (chan_at * blocks + block_at) * chunk
    place = jnp.stack([valid_len[0], base, chan_at, block_at, shard_base]).astype(jnp.int32)

    both = jnp.concatenate(
        [signal.reshape(peers, chunk, part), skip_in.reshape(peers, chunk, part)], axis=2
    )
    both = lax.all_to_all(both, ("chan", "blk"), 0, 0, tiled=True)

    vmem = pl.BlockSpec(memory_space=pltpu.VMEM)
    smem = pl.BlockSpec(memory_space=pltpu.SMEM)
    shape = jax.ShapeDtypeStruct
    filters, gates, skip_sum, pool = pl.pallas_call(
        lambda *refs: forward_kernel(blocks, chunk, *refs),
        out_shape=(
            shape((layers, rows, width), F32),
            shape((layers, rows, width), F32),
            shape((rows, width), F32),
            shape((blocks, blocks + 8, width), F32),
        ),
        in_specs=[smem, smem, smem] + [vmem] * 5,
        out_specs=(vmem,) * 4,
        compiler_params=pltpu.CompilerParams(vmem_limit_bytes=32 << 20),
        name="forward",
    )(place, event_bin, observed, both, tap_weight, tap_bias, res_weight, skip_weight)

    pool = lax.all_to_all(pool, "blk", 0, 0, tiled=True)

    nll, grads = pl.pallas_call(
        lambda *refs: backward_kernel(blocks, chunk, *refs),
        out_shape=(
            shape((1, 2), F32),
            shape((chans, blocks, chunk, part), BF16),
        ),
        in_specs=[smem] + [vmem] * 11,
        out_specs=(vmem, vmem),
        scratch_shapes=[pltpu.VMEM((width + 8, 128), F32)],
        compiler_params=pltpu.CompilerParams(vmem_limit_bytes=32 << 20),
        name="backward",
    )(
        place,
        pool,
        filters,
        gates,
        skip_sum,
        tap_weight,
        res_weight,
        skip_weight,
        head_w1,
        head_b1.reshape(1, -1),
        head_w2,
        head_second_bias.reshape(1, -1),
    )
    grads = lax.all_to_all(
        grads.reshape(peers, chunk, part), ("chan", "blk"), 0, 0, tiled=True
    )
    return (nll.reshape(2), grads.reshape(shard_rows, part))


def solution(mesh):
    blocks = 16
    devices = mesh.devices
    split = Mesh(
        devices.reshape(blocks, devices.shape[0] // blocks, devices.shape[1]),
        ("blk", "j", "chan"),
    )
    time = ("blk", "j")
    return jax.shard_map(
        local,
        mesh=split,
        in_specs=(
            P(time, "chan"),
            P(time, "chan"),
            P(),
            P(),
            P(),
            P(),
            P(),
            P(),
            P(),
            P(),
            P(time),
            P(time),
            P(),
        ),
        out_specs=(P(("blk", "j", "chan")), P(time, "chan")),
        check_vma=False,
    )
```

```python
import jax
import jax.numpy as jnp
from jax import lax
from jax.experimental import pallas as pl
from jax.experimental.pallas import tpu as pltpu
from jax.sharding import Mesh
from jax.sharding import PartitionSpec as P

WLEN = 128
FIRST_DILATION = 8192
F32 = jnp.float32
BF16 = jnp.bfloat16
EXACT = lax.Precision.HIGHEST


def dot(a, b):
    return jnp.dot(a, b, preferred_element_type=F32)


def dot_t(a, b, precision=None):
    return lax.dot_general(
        a, b, (((1,), (1,)), ((), ())), preferred_element_type=F32, precision=precision
    )


def sigmoid(v):
    return 0.5 * jnp.tanh(0.5 * v) + 0.5


def row_keep(limit, base, blocks, chunk, width):
    rows = lax.broadcasted_iota(jnp.int32, (blocks * chunk, width), 0)
    position = (rows // chunk) * FIRST_DILATION + rows % chunk + base
    return position < limit


def start_all(copies):
    for copy in copies:
        copy.start()


def wait_all(copies):
    for copy in copies:
        copy.wait()


def join_kernel(signal_ref, skip_ref, both_ref, sems):
    copies = [
        pltpu.make_async_copy(signal_ref, both_ref.at[:, 0], sems.at[0]),
        pltpu.make_async_copy(skip_ref, both_ref.at[:, 1], sems.at[1]),
    ]
    start_all(copies)
    wait_all(copies)


def forward_kernel(
    blocks,
    chunk,
    place_ref,
    both_ref,
    tap_hbm,
    bias_hbm,
    res_hbm,
    skipw_hbm,
    act_hbm,
    skip_hbm,
    pool_hbm,
    tap_ref,
    bias_ref,
    res_ref,
    skipw_ref,
    act_ref,
    skip_ref,
    pool_ref,
    in_sems,
    out_sems,
):
    layers = tap_ref.shape[0]
    part = both_ref.shape[3]
    width = 2 * part
    rows = blocks * chunk
    limit, base, chan_at = place_ref[0], place_ref[1], place_ref[2]
    taps = [
        pltpu.make_async_copy(tap_hbm.at[k], tap_ref.at[k], in_sems.at[k]) for k in range(layers)
    ]
    skips = [
        pltpu.make_async_copy(skipw_hbm.at[k], skipw_ref.at[k], in_sems.at[layers + k])
        for k in range(layers)
    ]
    ress = [
        pltpu.make_async_copy(res_hbm.at[k], res_ref.at[k], in_sems.at[2 * layers + k])
        for k in range(layers - 1)
    ]
    bias_copy = pltpu.make_async_copy(bias_hbm, bias_ref, in_sems.at[3 * layers])
    outs = []
    start_all([taps[0], bias_copy, ress[0], skips[0]])
    for k in range(1, layers):
        start_all([taps[k]] + ress[k : k + 1] + [skips[k]])
    current = jnp.concatenate(
        [
            both_ref[:blocks, 0].reshape(rows, part),
            both_ref[blocks:, 0].reshape(rows, part),
        ],
        axis=1,
    )
    skip_sum = jnp.concatenate(
        [
            both_ref[:blocks, 1].reshape(rows, part),
            both_ref[blocks:, 1].reshape(rows, part),
        ],
        axis=1,
    ).astype(F32)
    bias_copy.wait()
    for layer in range(layers):
        taps[layer].wait()
        late = chunk * 2**layer
        delayed = jnp.concatenate(
            [jnp.zeros((late, width), BF16), current[: rows - late]], axis=0
        )
        preact = (
            dot(delayed, tap_ref[layer, 0])
            + dot(current, tap_ref[layer, 1])
            + bias_ref[layer : layer + 1, :]
        )
        filters = jnp.tanh(preact[:, :width])
        gates = sigmoid(preact[:, width:])
        act_ref[layer, 0] = filters
        act_ref[layer, 1] = gates
        outs.append(
            pltpu.make_async_copy(act_ref.at[layer], act_hbm.at[layer], out_sems.at[layer])
        )
        outs[-1].start()
        gated = (filters * gates).astype(BF16)
        skips[layer].wait()
        if layer < layers - 1:
            ress[layer].wait()
            current = (current.astype(F32) + dot(gated, res_ref[layer])).astype(BF16)
        skip_sum = skip_sum + dot(gated, skipw_ref[layer])
    skip_ref[...] = skip_sum
    outs.append(pltpu.make_async_copy(skip_ref, skip_hbm, out_sems.at[layers]))
    outs[-1].start()
    keep = row_keep(limit, base, blocks, chunk, width)
    active = jnp.where(keep, skip_sum * sigmoid(skip_sum), 0.0)
    sums = active.reshape(blocks, chunk, width).sum(axis=1)
    first = 5 + 2 * chan_at
    line = lax.broadcasted_iota(jnp.int32, (8, width), 0)
    bins = [place_ref[first + i].astype(F32) for i in (0, 1, 4, 5)]
    extra = jnp.where(
        line == 0,
        bins[0],
        jnp.where(line == 1, bins[1], jnp.where(line == 2, bins[2], bins[3])),
    )
    sums = sums.astype(BF16)
    extra = extra.astype(BF16)
    for other in range(blocks):
        pool_ref[other, :blocks, :] = sums
        pool_ref[other, blocks:, :] = extra
    outs.append(pltpu.make_async_copy(pool_ref, pool_hbm, out_sems.at[layers + 1]))
    outs[-1].start()
    wait_all(outs)


def mixture(params, log_time, seen, mixes):
    lanes = params.shape[1]
    lane = lax.broadcasted_iota(jnp.int32, params.shape, 1)
    valid = lane < mixes
    bend_logit = jnp.tanh(params)
    log_scale = jnp.tanh(pltpu.roll(params, lanes - mixes, 1))
    bend_shape = jnp.tanh(pltpu.roll(params, lanes - 2 * mixes, 1))
    logits = 4.0 * bend_logit
    raised = jnp.where(valid, jnp.exp(logits), 0.0)
    total = jnp.sum(raised, axis=1, keepdims=True)
    log_weight = logits - jnp.log(total)
    log_shape = 0.5 * bend_shape
    shape = jnp.exp(log_shape)
    ratio = log_time - log_scale
    power = jnp.exp(shape * ratio)
    density = log_shape - log_scale + (shape - 1.0) * ratio - power
    component = jnp.where(seen, density, -power)
    likely = jnp.where(valid, jnp.exp(log_weight + component), 0.0)
    mass = jnp.sum(likely, axis=1, keepdims=True)
    nll = -jnp.log(mass)
    owned = likely / mass
    to_logit = (raised / total - owned) * 4.0 * (1.0 - bend_logit * bend_logit)
    steep = power * shape
    to_scale = jnp.where(seen, steep - shape, steep)
    to_shape = jnp.where(seen, 1.0 + shape * ratio, 0.0) - steep * ratio
    to_scale = -owned * to_scale * (1.0 - log_scale * log_scale)
    to_shape = -owned * to_shape * 0.5 * (1.0 - bend_shape * bend_shape)
    zero = jnp.zeros_like(params)
    grad = (
        jnp.where(valid, to_logit, zero)
        + pltpu.roll(jnp.where(valid, to_scale, zero), mixes, 1)
        + pltpu.roll(jnp.where(valid, to_shape, zero), 2 * mixes, 1)
    )
    return nll, grad


def backward_kernel(
    blocks,
    chunk,
    place_ref,
    pool_ref,
    act_hbm,
    skip_hbm,
    tap_hbm,
    res_hbm,
    skipw_hbm,
    head1_ref,
    headb1_ref,
    head2_ref,
    headb2_ref,
    nll_ref,
    grad_ref,
    act_ref,
    skip_ref,
    tap_ref,
    res_ref,
    skipw_ref,
    pad_ref,
    sems,
):
    layers = tap_ref.shape[0]
    width = skip_ref.shape[1]
    skip_copy = pltpu.make_async_copy(skip_hbm, skip_ref, sems.at[0])

    def loads(k):
        copies = [
            pltpu.make_async_copy(skipw_hbm.at[k], skipw_ref.at[k], sems.at[1 + 4 * k]),
            pltpu.make_async_copy(act_hbm.at[k], act_ref.at[k], sems.at[2 + 4 * k]),
            pltpu.make_async_copy(tap_hbm.at[k], tap_ref.at[k], sems.at[3 + 4 * k]),
        ]
        if k < layers - 1:
            copies.append(
                pltpu.make_async_copy(res_hbm.at[k], res_ref.at[k], sems.at[4 + 4 * k])
            )
        return copies

    layer_copies = [loads(k) for k in range(layers)]
    skip_copy.start()
    for k in range(layers - 1, -1, -1):
        start_all(layer_copies[k])
    part = width // 2
    rows = blocks * chunk
    lanes = pad_ref.shape[1]
    outs = head2_ref.shape[1]
    limit, base, chan_at, block_at, shard_base = (place_ref[i] for i in range(5))
    half = blocks // 2
    received = pool_ref[...].astype(F32)
    sums = jnp.concatenate(
        [
            received[:half, :blocks, :].sum(axis=0),
            received[half:, :blocks, :].sum(axis=0),
        ],
        axis=0,
    )
    bins = jnp.concatenate([received[:, blocks, :lanes], received[:, blocks + 1, :lanes]], axis=0)
    seen = (
        jnp.concatenate(
            [received[:, blocks + 2, :lanes], received[:, blocks + 3, :lanes]], axis=0
        )
        == 1.0
    )
    log_time = jnp.log((bins + 1.0) / 8.0)
    window = lax.broadcasted_iota(jnp.int32, (2 * blocks, width), 0)
    start = (
        (window % blocks) * FIRST_DILATION
        + shard_base
        + (2 * chan_at + window // blocks) * WLEN
    )
    count = jnp.clip(limit - start, 1, WLEN).astype(F32)
    pooled = sums / count
    pad_ref[...] = jnp.zeros_like(pad_ref)
    pad_ref[:width, :outs] = head2_ref[...]
    pad_ref[width : width + 1, :outs] = headb2_ref[...]
    head2 = pad_ref[:width, :]
    inner = (
        jnp.dot(pooled, head1_ref[...], preferred_element_type=F32, precision=EXACT)
        + headb1_ref[...]
    )
    open_inner = sigmoid(inner)
    hidden = inner * open_inner
    params = (
        jnp.dot(hidden, head2, preferred_element_type=F32, precision=EXACT)
        + pad_ref[width : width + 1, :]
    )
    nll, to_params = mixture(params, log_time, seen, outs // 3)
    to_hidden = dot_t(to_params, head2, EXACT)
    to_inner = to_hidden * open_inner * (1.0 + inner * (1.0 - open_inner))
    to_pooled = dot_t(to_inner, head1_ref[...], EXACT)

    row = lax.broadcasted_iota(jnp.int32, (2 * blocks, 2), 0)
    col = lax.broadcasted_iota(jnp.int32, (2 * blocks, 2), 1)
    mine = row == col * blocks + block_at
    nll_ref[...] = jnp.sum(jnp.where(mine, nll, 0.0), axis=0, keepdims=True)

    own_pool = jnp.where(block_at < half, to_pooled[:blocks], to_pooled[blocks:])
    spread = jnp.broadcast_to(own_pool[:, None, :], (blocks, chunk, width)).reshape(rows, width)
    keep = row_keep(limit, base, blocks, chunk, width)
    skip_copy.wait()
    skip_sum = skip_ref[...]
    sig = sigmoid(skip_sum)
    slope = sig * (1.0 + skip_sum * (1.0 - sig))
    grad_skip = jnp.where(keep, spread * slope, 0.0).astype(BF16)
    grad_rows = None
    for layer in range(layers - 1, -1, -1):
        early = chunk * 2**layer
        wait_all(layer_copies[layer])
        grad_gated = dot_t(grad_skip, skipw_ref[layer])
        if grad_rows is not None:
            grad_gated = grad_gated + dot_t(grad_rows, res_ref[layer])
        filters = act_ref[layer, 0]
        gates = act_ref[layer, 1]
        through = grad_gated * gates
        to_filter = (through * (1.0 - filters * filters)).astype(BF16)
        to_gate = (through * filters * (1.0 - gates)).astype(BF16)
        preact_grad = jnp.concatenate([to_filter, to_gate], axis=1)
        ahead = jnp.concatenate(
            [preact_grad[early:], jnp.zeros((early, 2 * width), BF16)], axis=0
        )
        summed = dot_t(preact_grad, tap_ref[layer, 1]) + dot_t(ahead, tap_ref[layer, 0])
        if grad_rows is not None:
            summed = summed + grad_rows.astype(F32)
        grad_rows = summed.astype(BF16)
    grad_ref[0] = grad_rows[:, :part].reshape(blocks, chunk, part)
    grad_ref[1] = grad_rows[:, part:].reshape(blocks, chunk, part)


def local(
    signal,
    skip_in,
    tap_weight,
    tap_bias,
    res_weight,
    skip_weight,
    head_w1,
    head_b1,
    head_w2,
    head_second_bias,
    event_bin,
    observed,
    valid_len,
):
    blocks = lax.axis_size("blk")
    chans = lax.axis_size("chan")
    shard_rows, part = signal.shape
    width = part * chans
    peers = blocks * chans
    chunk = shard_rows // peers
    rows = blocks * chunk
    layers = tap_weight.shape[0]
    block_at = lax.axis_index("blk")
    chan_at = lax.axis_index("chan")
    shard_base = lax.axis_index("j") * shard_rows
    base = shard_base + (chan_at * blocks + block_at) * chunk
    here = jnp.stack([base, chan_at, block_at, shard_base]).astype(jnp.int32)
    place = jnp.concatenate([valid_len, here, event_bin, observed])

    shape = jax.ShapeDtypeStruct
    vmem = pl.BlockSpec(memory_space=pltpu.VMEM)
    smem = pl.BlockSpec(memory_space=pltpu.SMEM)
    hbm = pl.BlockSpec(memory_space=pltpu.HBM)
    params = pltpu.CompilerParams(vmem_limit_bytes=24 << 20)

    def stay(array):
        return pltpu.with_memory_space_constraint(array, pltpu.HBM)


    both = pl.pallas_call(
        join_kernel,
        out_shape=shape((peers, 2, chunk, part), BF16),
        in_specs=[hbm, hbm],
        out_specs=hbm,
        scratch_shapes=[pltpu.SemaphoreType.DMA((2,))],
        compiler_params=params,
        name="join",
    )(stay(signal.reshape(peers, chunk, part)), stay(skip_in.reshape(peers, chunk, part)))
    both = lax.all_to_all(both, ("chan", "blk"), 0, 0, tiled=True)

    acts, skip_sum, pool = pl.pallas_call(
        lambda *refs: forward_kernel(blocks, chunk, *refs),
        out_shape=(
            pltpu.HBM((layers, 2, rows, width), F32),
            pltpu.HBM((rows, width), F32),
            pltpu.HBM((blocks, blocks + 8, width), BF16),
        ),
        in_specs=[smem, vmem] + [hbm] * 4,
        out_specs=(hbm,) * 3,
        scratch_shapes=[
            pltpu.VMEM(tap_weight.shape, BF16),
            pltpu.VMEM(tap_bias.shape, F32),
            pltpu.VMEM(res_weight.shape, BF16),
            pltpu.VMEM(skip_weight.shape, BF16),
            pltpu.VMEM((layers, 2, rows, width), F32),
            pltpu.VMEM((rows, width), F32),
            pltpu.VMEM((blocks, blocks + 8, width), BF16),
            pltpu.SemaphoreType.DMA((3 * layers + 1,)),
            pltpu.SemaphoreType.DMA((layers + 2,)),
        ],
        compiler_params=params,
        name="forward",
    )(
        place,
        both,
        stay(tap_weight),
        stay(tap_bias),
        stay(res_weight),
        stay(skip_weight),
    )

    pool = lax.all_to_all(pool, "blk", 0, 0, tiled=True)

    head_b1 = head_b1.reshape(1, -1)
    head_second_bias = head_second_bias.reshape(1, -1)
    nll, grads = pl.pallas_call(
        lambda *refs: backward_kernel(blocks, chunk, *refs),
        out_shape=(
            shape((1, 2), F32),
            shape((chans, blocks, chunk, part), BF16),
        ),
        in_specs=[smem, vmem] + [hbm] * 5 + [vmem] * 4,
        out_specs=(vmem, vmem),
        scratch_shapes=[
            pltpu.VMEM((layers, 2, rows, width), F32),
            pltpu.VMEM((rows, width), F32),
            pltpu.VMEM(tap_weight.shape, BF16),
            pltpu.VMEM(res_weight.shape, BF16),
            pltpu.VMEM(skip_weight.shape, BF16),
            pltpu.VMEM((width + 8, 128), F32),
            pltpu.SemaphoreType.DMA((1 + 4 * layers,)),
        ],
        compiler_params=params,
        name="backward",
    )(
        place,
        pool,
        stay(acts),
        stay(skip_sum),
        stay(tap_weight),
        stay(res_weight),
        stay(skip_weight),
        head_w1,
        head_b1,
        head_w2,
        head_second_bias,
    )
    grads = lax.all_to_all(
        grads.reshape(peers, chunk, part), ("chan", "blk"), 0, 0, tiled=True
    )
    return (nll.reshape(2), grads.reshape(shard_rows, part))


def solution(mesh):
    blocks = 16
    devices = mesh.devices
    split = Mesh(
        devices.reshape(blocks, devices.shape[0] // blocks, devices.shape[1]),
        ("blk", "j", "chan"),
    )
    time = ("blk", "j")
    return jax.shard_map(
        local,
        mesh=split,
        in_specs=(
            P(time, "chan"),
            P(time, "chan"),
            P(),
            P(),
            P(),
            P(),
            P(),
            P(),
            P(),
            P(),
            P(time),
            P(time),
            P(),
        ),
        out_specs=(P(("blk", "j", "chan")), P(time, "chan")),
        check_vma=False,
    )
```

```python
import jax
import jax.numpy as jnp
from jax import lax
from jax.experimental import pallas as pl
from jax.experimental.pallas import tpu as pltpu
from jax.sharding import Mesh
from jax.sharding import PartitionSpec as P

WLEN = 128
FIRST_DILATION = 8192
F32 = jnp.float32
BF16 = jnp.bfloat16
EXACT = lax.Precision.HIGHEST


def dot(a, b):
    return jnp.dot(a, b, preferred_element_type=F32)


def dot_t(a, b, precision=None):
    return lax.dot_general(
        a, b, (((1,), (1,)), ((), ())), preferred_element_type=F32, precision=precision
    )


def sigmoid(v):
    return 0.5 * jnp.tanh(0.5 * v) + 0.5


def position(blocks, chunk, chans):
    chan_at = lax.axis_index("chan")
    block_at = lax.axis_index("blk")
    shard_base = lax.axis_index("j") * (blocks * chans * chunk)
    base = shard_base + (chan_at * blocks + block_at) * chunk
    return base, chan_at, block_at, shard_base


def row_keep(limit, base, blocks, chunk, width):
    rows = lax.broadcasted_iota(jnp.int32, (blocks * chunk, width), 0)
    position = (rows // chunk) * FIRST_DILATION + rows % chunk + base
    return position < limit


def start_all(copies):
    for copy in copies:
        copy.start()


def wait_all(copies):
    for copy in copies:
        copy.wait()


def join_kernel(signal_ref, skip_ref, both_ref, sems):
    copies = [
        pltpu.make_async_copy(signal_ref, both_ref.at[:, 0], sems.at[0]),
        pltpu.make_async_copy(skip_ref, both_ref.at[:, 1], sems.at[1]),
    ]
    start_all(copies)
    wait_all(copies)


def forward_kernel(
    blocks,
    chunk,
    limit_hbm,
    bin_hbm,
    seen_hbm,
    both_ref,
    tap_ref,
    bias_ref,
    res_ref,
    skipw_ref,
    act_hbm,
    skip_hbm,
    pool_hbm,
    limit_ref,
    bin_ref,
    seen_ref,
    act_ref,
    skip_ref,
    pool_ref,
    in_sems,
    out_sems,
):
    layers = tap_ref.shape[0]
    part = both_ref.shape[3]
    width = 2 * part
    rows = blocks * chunk
    base, chan_at, _, _ = position(blocks, chunk, 2)
    scalars = [
        pltpu.make_async_copy(limit_hbm, limit_ref, in_sems.at[0]),
        pltpu.make_async_copy(bin_hbm, bin_ref, in_sems.at[1]),
        pltpu.make_async_copy(seen_hbm, seen_ref, in_sems.at[2]),
    ]
    start_all(scalars)
    outs = []
    current = jnp.concatenate(
        [
            both_ref[:blocks, 0].reshape(rows, part),
            both_ref[blocks:, 0].reshape(rows, part),
        ],
        axis=1,
    )
    skip_sum = jnp.concatenate(
        [
            both_ref[:blocks, 1].reshape(rows, part),
            both_ref[blocks:, 1].reshape(rows, part),
        ],
        axis=1,
    ).astype(F32)
    for layer in range(layers):
        late = chunk * 2**layer
        delayed = jnp.concatenate(
            [jnp.zeros((late, width), BF16), current[: rows - late]], axis=0
        )
        preact = (
            dot(delayed, tap_ref[layer, 0])
            + dot(current, tap_ref[layer, 1])
            + bias_ref[layer : layer + 1, :]
        )
        filters = jnp.tanh(preact[:, :width])
        gates = sigmoid(preact[:, width:])
        act_ref[layer, 0] = filters
        act_ref[layer, 1] = gates
        outs.append(
            pltpu.make_async_copy(act_ref.at[layer], act_hbm.at[layer], out_sems.at[layer])
        )
        outs[-1].start()
        gated = (filters * gates).astype(BF16)
        if layer < layers - 1:
            current = (current.astype(F32) + dot(gated, res_ref[layer])).astype(BF16)
        skip_sum = skip_sum + dot(gated, skipw_ref[layer])
    skip_ref[...] = skip_sum
    outs.append(pltpu.make_async_copy(skip_ref, skip_hbm, out_sems.at[layers]))
    outs[-1].start()
    wait_all(scalars)
    limit = limit_ref[0]
    keep = row_keep(limit, base, blocks, chunk, width)
    active = jnp.where(keep, skip_sum * sigmoid(skip_sum), 0.0)
    sums = active.reshape(blocks, chunk, width).sum(axis=1)
    first = 2 * chan_at
    line = lax.broadcasted_iota(jnp.int32, (8, width), 0)
    bins = [ref[first + i].astype(F32) for ref in (bin_ref, seen_ref) for i in (0, 1)]
    extra = jnp.where(
        line == 0,
        bins[0],
        jnp.where(line == 1, bins[1], jnp.where(line == 2, bins[2], bins[3])),
    )
    sums = sums.astype(BF16)
    extra = extra.astype(BF16)
    for other in range(blocks):
        pool_ref[other, :blocks, :] = sums
        pool_ref[other, blocks:, :] = extra
    outs.append(pltpu.make_async_copy(pool_ref, pool_hbm, out_sems.at[layers + 1]))
    outs[-1].start()
    wait_all(outs)


def mixture(params, log_time, seen, mixes):
    lanes = params.shape[1]
    lane = lax.broadcasted_iota(jnp.int32, params.shape, 1)
    valid = lane < mixes
    bend_logit = jnp.tanh(params)
    log_scale = jnp.tanh(pltpu.roll(params, lanes - mixes, 1))
    bend_shape = jnp.tanh(pltpu.roll(params, lanes - 2 * mixes, 1))
    logits = 4.0 * bend_logit
    raised = jnp.where(valid, jnp.exp(logits), 0.0)
    total = jnp.sum(raised, axis=1, keepdims=True)
    log_weight = logits - jnp.log(total)
    log_shape = 0.5 * bend_shape
    shape = jnp.exp(log_shape)
    ratio = log_time - log_scale
    power = jnp.exp(shape * ratio)
    density = log_shape - log_scale + (shape - 1.0) * ratio - power
    component = jnp.where(seen, density, -power)
    likely = jnp.where(valid, jnp.exp(log_weight + component), 0.0)
    mass = jnp.sum(likely, axis=1, keepdims=True)
    nll = -jnp.log(mass)
    owned = likely / mass
    to_logit = (raised / total - owned) * 4.0 * (1.0 - bend_logit * bend_logit)
    steep = power * shape
    to_scale = jnp.where(seen, steep - shape, steep)
    to_shape = jnp.where(seen, 1.0 + shape * ratio, 0.0) - steep * ratio
    to_scale = -owned * to_scale * (1.0 - log_scale * log_scale)
    to_shape = -owned * to_shape * 0.5 * (1.0 - bend_shape * bend_shape)
    zero = jnp.zeros_like(params)
    grad = (
        jnp.where(valid, to_logit, zero)
        + pltpu.roll(jnp.where(valid, to_scale, zero), mixes, 1)
        + pltpu.roll(jnp.where(valid, to_shape, zero), 2 * mixes, 1)
    )
    return nll, grad


def backward_kernel(
    blocks,
    chunk,
    limit_hbm,
    pool_ref,
    act_hbm,
    skip_hbm,
    tap_ref,
    res_ref,
    skipw_ref,
    head1_hbm,
    headb1_ref,
    head2_ref,
    headb2_ref,
    nll_ref,
    grad_ref,
    limit_ref,
    act_ref,
    skip_ref,
    head1_ref,
    pad_ref,
    sems,
):
    layers = tap_ref.shape[0]
    width = skip_ref.shape[1]
    skip_copy = pltpu.make_async_copy(skip_hbm, skip_ref, sems.at[0])

    act_copies = [
        pltpu.make_async_copy(act_hbm.at[k], act_ref.at[k], sems.at[1 + k]) for k in range(layers)
    ]
    head_copy = pltpu.make_async_copy(head1_hbm, head1_ref, sems.at[1 + layers])
    limit_copy = pltpu.make_async_copy(limit_hbm, limit_ref, sems.at[2 + layers])
    limit_copy.start()
    head_copy.start()
    skip_copy.start()
    for k in range(layers - 1, -1, -1):
        act_copies[k].start()
    part = width // 2
    rows = blocks * chunk
    lanes = pad_ref.shape[1]
    outs = head2_ref.shape[1]
    base, chan_at, block_at, shard_base = position(blocks, chunk, 2)
    half = blocks // 2
    received = pool_ref[...].astype(F32)
    sums = jnp.concatenate(
        [
            received[:half, :blocks, :].sum(axis=0),
            received[half:, :blocks, :].sum(axis=0),
        ],
        axis=0,
    )
    bins = jnp.concatenate([received[:, blocks, :lanes], received[:, blocks + 1, :lanes]], axis=0)
    seen = (
        jnp.concatenate(
            [received[:, blocks + 2, :lanes], received[:, blocks + 3, :lanes]], axis=0
        )
        == 1.0
    )
    log_time = jnp.log((bins + 1.0) / 8.0)
    window = lax.broadcasted_iota(jnp.int32, (2 * blocks, width), 0)
    start = (
        (window % blocks) * FIRST_DILATION
        + shard_base
        + (2 * chan_at + window // blocks) * WLEN
    )
    limit_copy.wait()
    limit = limit_ref[0]
    count = jnp.clip(limit - start, 1, WLEN).astype(F32)
    pooled = sums / count
    pad_ref[...] = jnp.zeros_like(pad_ref)
    pad_ref[:width, :outs] = head2_ref[...]
    pad_ref[width : width + 1, :outs] = headb2_ref[...]
    head2 = pad_ref[:width, :]
    head_copy.wait()
    inner = (
        jnp.dot(pooled, head1_ref[...], preferred_element_type=F32, precision=EXACT)
        + headb1_ref[...]
    )
    open_inner = sigmoid(inner)
    hidden = inner * open_inner
    params = (
        jnp.dot(hidden, head2, preferred_element_type=F32, precision=EXACT)
        + pad_ref[width : width + 1, :]
    )
    nll, to_params = mixture(params, log_time, seen, outs // 3)
    to_hidden = dot_t(to_params, head2, EXACT)
    to_inner = to_hidden * open_inner * (1.0 + inner * (1.0 - open_inner))
    to_pooled = dot_t(to_inner, head1_ref[...], EXACT)

    row = lax.broadcasted_iota(jnp.int32, (2 * blocks, 2), 0)
    col = lax.broadcasted_iota(jnp.int32, (2 * blocks, 2), 1)
    mine = row == col * blocks + block_at
    nll_ref[...] = jnp.sum(jnp.where(mine, nll, 0.0), axis=0, keepdims=True)

    own_pool = jnp.where(block_at < half, to_pooled[:blocks], to_pooled[blocks:])
    spread = jnp.broadcast_to(own_pool[:, None, :], (blocks, chunk, width)).reshape(rows, width)
    keep = row_keep(limit, base, blocks, chunk, width)
    skip_copy.wait()
    skip_sum = skip_ref[...]
    sig = sigmoid(skip_sum)
    slope = sig * (1.0 + skip_sum * (1.0 - sig))
    grad_skip = jnp.where(keep, spread * slope, 0.0).astype(BF16)
    grad_rows = None
    for layer in range(layers - 1, -1, -1):
        early = chunk * 2**layer
        act_copies[layer].wait()
        grad_gated = dot_t(grad_skip, skipw_ref[layer])
        if grad_rows is not None:
            grad_gated = grad_gated + dot_t(grad_rows, res_ref[layer])
        filters = act_ref[layer, 0]
        gates = act_ref[layer, 1]
        through = grad_gated * gates
        to_filter = (through * (1.0 - filters * filters)).astype(BF16)
        to_gate = (through * filters * (1.0 - gates)).astype(BF16)
        preact_grad = jnp.concatenate([to_filter, to_gate], axis=1)
        ahead = jnp.concatenate(
            [preact_grad[early:], jnp.zeros((early, 2 * width), BF16)], axis=0
        )
        summed = dot_t(preact_grad, tap_ref[layer, 1]) + dot_t(ahead, tap_ref[layer, 0])
        if grad_rows is not None:
            summed = summed + grad_rows.astype(F32)
        grad_rows = summed.astype(BF16)
    grad_ref[0] = grad_rows[:, :part].reshape(blocks, chunk, part)
    grad_ref[1] = grad_rows[:, part:].reshape(blocks, chunk, part)


def local(
    signal,
    skip_in,
    tap_weight,
    tap_bias,
    res_weight,
    skip_weight,
    head_w1,
    head_b1,
    head_w2,
    head_second_bias,
    event_bin,
    observed,
    valid_len,
):
    blocks = lax.axis_size("blk")
    chans = lax.axis_size("chan")
    shard_rows, part = signal.shape
    width = part * chans
    peers = blocks * chans
    chunk = shard_rows // peers
    rows = blocks * chunk
    layers = tap_weight.shape[0]
    shape = jax.ShapeDtypeStruct
    vmem = pl.BlockSpec(memory_space=pltpu.VMEM)
    hbm = pl.BlockSpec(memory_space=pltpu.HBM)
    params = pltpu.CompilerParams(vmem_limit_bytes=24 << 20)

    def stay(array):
        return pltpu.with_memory_space_constraint(array, pltpu.HBM)


    both = pl.pallas_call(
        join_kernel,
        out_shape=shape((peers, 2, chunk, part), BF16),
        in_specs=[hbm, hbm],
        out_specs=vmem,
        scratch_shapes=[pltpu.SemaphoreType.DMA((2,))],
        compiler_params=params,
        cost_estimate=pl.CostEstimate(
            flops=40_000_000_000, bytes_accessed=2 * peers * chunk * part * 4, transcendentals=0
        ),
        name="join",
    )(stay(signal.reshape(peers, chunk, part)), stay(skip_in.reshape(peers, chunk, part)))
    both = lax.all_to_all(both, ("chan", "blk"), 0, 0, tiled=True)

    acts, skip_sum, pool = pl.pallas_call(
        lambda *refs: forward_kernel(blocks, chunk, *refs),
        out_shape=(
            pltpu.HBM((layers, 2, rows, width), F32),
            pltpu.HBM((rows, width), F32),
            pltpu.HBM((blocks, blocks + 8, width), BF16),
        ),
        in_specs=[hbm] * 3 + [vmem] * 5,
        out_specs=(hbm,) * 3,
        scratch_shapes=[
            pltpu.SMEM(valid_len.shape, jnp.int32),
            pltpu.SMEM(event_bin.shape, jnp.int32),
            pltpu.SMEM(observed.shape, jnp.int32),
            pltpu.VMEM((layers, 2, rows, width), F32),
            pltpu.VMEM((rows, width), F32),
            pltpu.VMEM((blocks, blocks + 8, width), BF16),
            pltpu.SemaphoreType.DMA((3,)),
            pltpu.SemaphoreType.DMA((layers + 2,)),
        ],
        compiler_params=params,
        cost_estimate=pl.CostEstimate(
            flops=40_000_000_000, bytes_accessed=8 << 20, transcendentals=0
        ),
        name="forward",
    )(
        valid_len,
        stay(event_bin),
        stay(observed),
        both,
        tap_weight,
        tap_bias,
        res_weight,
        skip_weight,
    )

    pool = lax.all_to_all(pool, "blk", 0, 0, tiled=True)

    head_b1 = head_b1.reshape(1, -1)
    head_second_bias = head_second_bias.reshape(1, -1)
    nll, grads = pl.pallas_call(
        lambda *refs: backward_kernel(blocks, chunk, *refs),
        out_shape=(
            shape((1, 2), F32),
            shape((chans, blocks, chunk, part), BF16),
        ),
        in_specs=[hbm, vmem] + [hbm] * 2 + [vmem] * 3 + [hbm] + [vmem] * 3,
        out_specs=(vmem, vmem),
        scratch_shapes=[
            pltpu.SMEM(valid_len.shape, jnp.int32),
            pltpu.VMEM((layers, 2, rows, width), F32),
            pltpu.VMEM((rows, width), F32),
            pltpu.VMEM(head_w1.shape, F32),
            pltpu.VMEM((width + 8, 128), F32),
            pltpu.SemaphoreType.DMA((3 + layers,)),
        ],
        compiler_params=params,
        name="backward",
    )(
        valid_len,
        pool,
        stay(acts),
        stay(skip_sum),
        tap_weight,
        res_weight,
        skip_weight,
        stay(head_w1),
        head_b1,
        head_w2,
        head_second_bias,
    )
    grads = lax.all_to_all(
        grads.reshape(peers, chunk, part), ("chan", "blk"), 0, 0, tiled=True
    )
    return (nll.reshape(2), grads.reshape(shard_rows, part))


def solution(mesh):
    blocks = 16
    devices = mesh.devices
    split = Mesh(
        devices.reshape(blocks, devices.shape[0] // blocks, devices.shape[1]),
        ("blk", "j", "chan"),
    )
    time = ("blk", "j")
    return jax.shard_map(
        local,
        mesh=split,
        in_specs=(
            P(time, "chan"),
            P(time, "chan"),
            P(),
            P(),
            P(),
            P(),
            P(),
            P(),
            P(),
            P(),
            P(time),
            P(time),
            P(),
        ),
        out_specs=(P(("blk", "j", "chan")), P(time, "chan")),
        check_vma=False,
    )
```

```python
import jax
import jax.numpy as jnp
from jax import lax
from jax.experimental import pallas as pl
from jax.experimental.pallas import tpu as pltpu
from jax.sharding import Mesh
from jax.sharding import PartitionSpec as P

WLEN = 128
FIRST_DILATION = 8192
F32 = jnp.float32
BF16 = jnp.bfloat16
FIRST = 26
EXACT = lax.Precision.HIGHEST


def dot(a, b):
    return jnp.dot(a, b, preferred_element_type=F32)


def dot_t(a, b, precision=None):
    return lax.dot_general(
        a, b, (((1,), (1,)), ((), ())), preferred_element_type=F32, precision=precision
    )


def sigmoid(v):
    return 0.5 * jnp.tanh(0.5 * v) + 0.5


def position(blocks, chunk, chans):
    chan_at = lax.axis_index("chan")
    block_at = lax.axis_index("blk")
    shard_base = lax.axis_index("j") * (blocks * chans * chunk)
    base = shard_base + (chan_at * blocks + block_at) * chunk
    return base, chan_at, block_at, shard_base


def row_keep(limit, base, blocks, chunk, width):
    rows = lax.broadcasted_iota(jnp.int32, (blocks * chunk, width), 0)
    position = (rows // chunk) * FIRST_DILATION + rows % chunk + base
    return position < limit


def start_all(copies):
    for copy in copies:
        copy.start()


def wait_all(copies):
    for copy in copies:
        copy.wait()


def turn(peers):
    lead = peers - FIRST
    return [(FIRST, 0, lead), (0, lead, FIRST)]


def join_kernel(signal_ref, skip_ref, both_ref, sems):
    copies = []
    for source, target, size in turn(both_ref.shape[0]):
        for part, ref in enumerate((signal_ref, skip_ref)):
            copies.append(
                pltpu.make_async_copy(
                    ref.at[pl.ds(source, size)],
                    both_ref.at[pl.ds(target, size), part],
                    sems.at[len(copies)],
                )
            )
    start_all(copies)
    wait_all(copies)


def place_kernel(received_ref, grad_hbm, sems):
    copies = []
    for target, source, size in turn(received_ref.shape[0]):
        copies.append(
            pltpu.make_async_copy(
                received_ref.at[pl.ds(source, size)],
                grad_hbm.at[pl.ds(target, size)],
                sems.at[len(copies)],
            )
        )
    start_all(copies)
    wait_all(copies)


def spans(start, size, total):
    start = (start - FIRST) % total
    head = min(size, total - start)
    return [(start, head)] + ([(0, size - head)] if head < size else [])


def read_turned(ref, start, size, part):
    pieces = [
        ref[at : at + count, part].reshape(count * ref.shape[2], ref.shape[3])
        for at, count in spans(start, size, ref.shape[0])
    ]
    return pieces[0] if len(pieces) == 1 else jnp.concatenate(pieces, axis=0)


def forward_kernel(
    blocks,
    chunk,
    limit_hbm,
    bin_hbm,
    seen_hbm,
    both_ref,
    tap_ref,
    bias_ref,
    res_ref,
    skipw_ref,
    act_hbm,
    skip_hbm,
    pool_hbm,
    limit_ref,
    bin_ref,
    seen_ref,
    act_ref,
    skip_ref,
    pool_ref,
    in_sems,
    out_sems,
):
    layers = tap_ref.shape[0]
    part = both_ref.shape[3]
    width = 2 * part
    rows = blocks * chunk
    base, chan_at, _, _ = position(blocks, chunk, 2)
    scalars = [
        pltpu.make_async_copy(limit_hbm, limit_ref, in_sems.at[0]),
        pltpu.make_async_copy(bin_hbm, bin_ref, in_sems.at[1]),
        pltpu.make_async_copy(seen_hbm, seen_ref, in_sems.at[2]),
    ]
    start_all(scalars)
    outs = []
    current, skip_sum = (
        jnp.concatenate(
            [read_turned(both_ref, c * blocks, blocks, part_at) for c in range(2)], axis=1
        )
        for part_at in range(2)
    )
    skip_sum = skip_sum.astype(F32)
    for layer in range(layers):
        late = chunk * 2**layer
        delayed = jnp.concatenate(
            [jnp.zeros((late, width), BF16), current[: rows - late]], axis=0
        )
        preact = (
            dot(delayed, tap_ref[layer, 0])
            + dot(current, tap_ref[layer, 1])
            + bias_ref[layer : layer + 1, :]
        )
        filters = jnp.tanh(preact[:, :width])
        gates = sigmoid(preact[:, width:])
        act_ref[layer, 0] = filters
        act_ref[layer, 1] = gates
        outs.append(
            pltpu.make_async_copy(act_ref.at[layer], act_hbm.at[layer], out_sems.at[layer])
        )
        outs[-1].start()
        gated = (filters * gates).astype(BF16)
        if layer < layers - 1:
            current = (current.astype(F32) + dot(gated, res_ref[layer])).astype(BF16)
        skip_sum = skip_sum + dot(gated, skipw_ref[layer])
    skip_ref[...] = skip_sum
    outs.append(pltpu.make_async_copy(skip_ref, skip_hbm, out_sems.at[layers]))
    outs[-1].start()
    wait_all(scalars)
    limit = limit_ref[0]
    keep = row_keep(limit, base, blocks, chunk, width)
    active = jnp.where(keep, skip_sum * sigmoid(skip_sum), 0.0)
    sums = active.reshape(blocks, chunk, width).sum(axis=1)
    first = 2 * chan_at
    line = lax.broadcasted_iota(jnp.int32, (8, width), 0)
    bins = [ref[first + i].astype(F32) for ref in (bin_ref, seen_ref) for i in (0, 1)]
    extra = jnp.where(
        line == 0,
        bins[0],
        jnp.where(line == 1, bins[1], jnp.where(line == 2, bins[2], bins[3])),
    )
    sums = sums.astype(BF16)
    extra = extra.astype(BF16)
    for other in range(blocks):
        pool_ref[other, :blocks, :] = sums
        pool_ref[other, blocks:, :] = extra
    outs.append(pltpu.make_async_copy(pool_ref, pool_hbm, out_sems.at[layers + 1]))
    outs[-1].start()
    wait_all(outs)


def mixture(params, log_time, seen, mixes):
    lanes = params.shape[1]
    lane = lax.broadcasted_iota(jnp.int32, params.shape, 1)
    valid = lane < mixes
    bend_logit = jnp.tanh(params)
    log_scale = jnp.tanh(pltpu.roll(params, lanes - mixes, 1))
    bend_shape = jnp.tanh(pltpu.roll(params, lanes - 2 * mixes, 1))
    logits = 4.0 * bend_logit
    raised = jnp.where(valid, jnp.exp(logits), 0.0)
    total = jnp.sum(raised, axis=1, keepdims=True)
    log_weight = logits - jnp.log(total)
    log_shape = 0.5 * bend_shape
    shape = jnp.exp(log_shape)
    ratio = log_time - log_scale
    power = jnp.exp(shape * ratio)
    density = log_shape - log_scale + (shape - 1.0) * ratio - power
    component = jnp.where(seen, density, -power)
    likely = jnp.where(valid, jnp.exp(log_weight + component), 0.0)
    mass = jnp.sum(likely, axis=1, keepdims=True)
    nll = -jnp.log(mass)
    owned = likely / mass
    to_logit = (raised / total - owned) * 4.0 * (1.0 - bend_logit * bend_logit)
    steep = power * shape
    to_scale = jnp.where(seen, steep - shape, steep)
    to_shape = jnp.where(seen, 1.0 + shape * ratio, 0.0) - steep * ratio
    to_scale = -owned * to_scale * (1.0 - log_scale * log_scale)
    to_shape = -owned * to_shape * 0.5 * (1.0 - bend_shape * bend_shape)
    zero = jnp.zeros_like(params)
    grad = (
        jnp.where(valid, to_logit, zero)
        + pltpu.roll(jnp.where(valid, to_scale, zero), mixes, 1)
        + pltpu.roll(jnp.where(valid, to_shape, zero), 2 * mixes, 1)
    )
    return nll, grad


def backward_kernel(
    blocks,
    chunk,
    limit_hbm,
    pool_ref,
    act_hbm,
    skip_hbm,
    tap_ref,
    res_ref,
    skipw_ref,
    head1_hbm,
    headb1_ref,
    head2_ref,
    headb2_ref,
    nll_ref,
    grad_ref,
    limit_ref,
    act_ref,
    skip_ref,
    head1_ref,
    pad_ref,
    sems,
):
    layers = tap_ref.shape[0]
    width = skip_ref.shape[1]
    skip_copy = pltpu.make_async_copy(skip_hbm, skip_ref, sems.at[0])

    act_copies = [
        pltpu.make_async_copy(act_hbm.at[k], act_ref.at[k], sems.at[1 + k]) for k in range(layers)
    ]
    head_copy = pltpu.make_async_copy(head1_hbm, head1_ref, sems.at[1 + layers])
    limit_copy = pltpu.make_async_copy(limit_hbm, limit_ref, sems.at[2 + layers])
    limit_copy.start()
    head_copy.start()
    skip_copy.start()
    for k in range(layers - 1, -1, -1):
        act_copies[k].start()
    part = width // 2
    rows = blocks * chunk
    lanes = pad_ref.shape[1]
    outs = head2_ref.shape[1]
    base, chan_at, block_at, shard_base = position(blocks, chunk, 2)
    half = blocks // 2
    received = pool_ref[...].astype(F32)
    first = FIRST % blocks
    received = jnp.concatenate([received[blocks - first :], received[: blocks - first]], axis=0)
    sums = jnp.concatenate(
        [
            received[:half, :blocks, :].sum(axis=0),
            received[half:, :blocks, :].sum(axis=0),
        ],
        axis=0,
    )
    bins = jnp.concatenate([received[:, blocks, :lanes], received[:, blocks + 1, :lanes]], axis=0)
    seen = (
        jnp.concatenate(
            [received[:, blocks + 2, :lanes], received[:, blocks + 3, :lanes]], axis=0
        )
        == 1.0
    )
    log_time = jnp.log((bins + 1.0) / 8.0)
    window = lax.broadcasted_iota(jnp.int32, (2 * blocks, width), 0)
    start = (
        (window % blocks) * FIRST_DILATION
        + shard_base
        + (2 * chan_at + window // blocks) * WLEN
    )
    limit_copy.wait()
    limit = limit_ref[0]
    count = jnp.clip(limit - start, 1, WLEN).astype(F32)
    pooled = sums / count
    pad_ref[...] = jnp.zeros_like(pad_ref)
    pad_ref[:width, :outs] = head2_ref[...]
    pad_ref[width : width + 1, :outs] = headb2_ref[...]
    head2 = pad_ref[:width, :]
    head_copy.wait()
    inner = (
        jnp.dot(pooled, head1_ref[...], preferred_element_type=F32, precision=EXACT)
        + headb1_ref[...]
    )
    open_inner = sigmoid(inner)
    hidden = inner * open_inner
    params = (
        jnp.dot(hidden, head2, preferred_element_type=F32, precision=EXACT)
        + pad_ref[width : width + 1, :]
    )
    nll, to_params = mixture(params, log_time, seen, outs // 3)
    to_hidden = dot_t(to_params, head2, EXACT)
    to_inner = to_hidden * open_inner * (1.0 + inner * (1.0 - open_inner))
    to_pooled = dot_t(to_inner, head1_ref[...], EXACT)

    row = lax.broadcasted_iota(jnp.int32, (2 * blocks, 2), 0)
    col = lax.broadcasted_iota(jnp.int32, (2 * blocks, 2), 1)
    mine = row == col * blocks + block_at
    nll_ref[...] = jnp.sum(jnp.where(mine, nll, 0.0), axis=0, keepdims=True)

    own_pool = jnp.where(block_at < half, to_pooled[:blocks], to_pooled[blocks:])
    spread = jnp.broadcast_to(own_pool[:, None, :], (blocks, chunk, width)).reshape(rows, width)
    keep = row_keep(limit, base, blocks, chunk, width)
    skip_copy.wait()
    skip_sum = skip_ref[...]
    sig = sigmoid(skip_sum)
    slope = sig * (1.0 + skip_sum * (1.0 - sig))
    grad_skip = jnp.where(keep, spread * slope, 0.0).astype(BF16)
    grad_rows = None
    for layer in range(layers - 1, -1, -1):
        early = chunk * 2**layer
        act_copies[layer].wait()
        grad_gated = dot_t(grad_skip, skipw_ref[layer])
        if grad_rows is not None:
            grad_gated = grad_gated + dot_t(grad_rows, res_ref[layer])
        filters = act_ref[layer, 0]
        gates = act_ref[layer, 1]
        through = grad_gated * gates
        to_filter = (through * (1.0 - filters * filters)).astype(BF16)
        to_gate = (through * filters * (1.0 - gates)).astype(BF16)
        preact_grad = jnp.concatenate([to_filter, to_gate], axis=1)
        ahead = jnp.concatenate(
            [preact_grad[early:], jnp.zeros((early, 2 * width), BF16)], axis=0
        )
        summed = dot_t(preact_grad, tap_ref[layer, 1]) + dot_t(ahead, tap_ref[layer, 0])
        if grad_rows is not None:
            summed = summed + grad_rows.astype(F32)
        grad_rows = summed.astype(BF16)
    peers = grad_ref.shape[0]
    for c in range(2):
        done = 0
        for at, count in spans(c * blocks, blocks, peers):
            piece = grad_rows[done * chunk : (done + count) * chunk, c * part : (c + 1) * part]
            grad_ref[at : at + count] = piece.reshape(count, chunk, part)
            done += count


def local(
    signal,
    skip_in,
    tap_weight,
    tap_bias,
    res_weight,
    skip_weight,
    head_w1,
    head_b1,
    head_w2,
    head_second_bias,
    event_bin,
    observed,
    valid_len,
):
    blocks = lax.axis_size("blk")
    chans = lax.axis_size("chan")
    shard_rows, part = signal.shape
    width = part * chans
    peers = blocks * chans
    chunk = shard_rows // peers
    rows = blocks * chunk
    layers = tap_weight.shape[0]
    shape = jax.ShapeDtypeStruct
    vmem = pl.BlockSpec(memory_space=pltpu.VMEM)
    hbm = pl.BlockSpec(memory_space=pltpu.HBM)
    params = pltpu.CompilerParams(vmem_limit_bytes=24 << 20)

    def stay(array):
        return pltpu.with_memory_space_constraint(array, pltpu.HBM)


    both = pl.pallas_call(
        join_kernel,
        out_shape=shape((peers, 2, chunk, part), BF16),
        in_specs=[hbm, hbm],
        out_specs=vmem,
        scratch_shapes=[pltpu.SemaphoreType.DMA((4,))],
        compiler_params=params,
        cost_estimate=pl.CostEstimate(
            flops=40_000_000_000, bytes_accessed=2 * peers * chunk * part * 4, transcendentals=0
        ),
        name="join",
    )(stay(signal.reshape(peers, chunk, part)), stay(skip_in.reshape(peers, chunk, part)))
    shards = lax.axis_size("j")
    everyone = ("blk", "j", "chan")
    order = [(FIRST + i) % peers for i in range(peers)]
    wide = [
        [((k % blocks) * shards + j) * chans + k // blocks for k in order] for j in range(shards)
    ]
    first = FIRST % blocks
    near = [[(first + i) % blocks for i in range(blocks)]]
    both = lax.all_to_all(both, everyone, 0, 0, tiled=True, axis_index_groups=wide)

    acts, skip_sum, pool = pl.pallas_call(
        lambda *refs: forward_kernel(blocks, chunk, *refs),
        out_shape=(
            pltpu.HBM((layers, 2, rows, width), F32),
            pltpu.HBM((rows, width), F32),
            pltpu.HBM((blocks, blocks + 8, width), BF16),
        ),
        in_specs=[hbm] * 3 + [vmem] * 5,
        out_specs=(hbm,) * 3,
        scratch_shapes=[
            pltpu.SMEM(valid_len.shape, jnp.int32),
            pltpu.SMEM(event_bin.shape, jnp.int32),
            pltpu.SMEM(observed.shape, jnp.int32),
            pltpu.VMEM((layers, 2, rows, width), F32),
            pltpu.VMEM((rows, width), F32),
            pltpu.VMEM((blocks, blocks + 8, width), BF16),
            pltpu.SemaphoreType.DMA((3,)),
            pltpu.SemaphoreType.DMA((layers + 2,)),
        ],
        compiler_params=params,
        cost_estimate=pl.CostEstimate(
            flops=40_000_000_000, bytes_accessed=8 << 20, transcendentals=0
        ),
        name="forward",
    )(
        valid_len,
        stay(event_bin),
        stay(observed),
        both,
        tap_weight,
        tap_bias,
        res_weight,
        skip_weight,
    )

    pool = lax.all_to_all(pool, "blk", 0, 0, tiled=True, axis_index_groups=near)

    head_b1 = head_b1.reshape(1, -1)
    head_second_bias = head_second_bias.reshape(1, -1)
    nll, grads = pl.pallas_call(
        lambda *refs: backward_kernel(blocks, chunk, *refs),
        out_shape=(
            shape((1, 2), F32),
            shape((peers, chunk, part), BF16),
        ),
        in_specs=[hbm, vmem] + [hbm] * 2 + [vmem] * 3 + [hbm] + [vmem] * 3,
        out_specs=(vmem, vmem),
        scratch_shapes=[
            pltpu.SMEM(valid_len.shape, jnp.int32),
            pltpu.VMEM((layers, 2, rows, width), F32),
            pltpu.VMEM((rows, width), F32),
            pltpu.VMEM(head_w1.shape, F32),
            pltpu.VMEM((width + 8, 128), F32),
            pltpu.SemaphoreType.DMA((3 + layers,)),
        ],
        compiler_params=params,
        name="backward",
    )(
        valid_len,
        pool,
        stay(acts),
        stay(skip_sum),
        tap_weight,
        res_weight,
        skip_weight,
        stay(head_w1),
        head_b1,
        head_w2,
        head_second_bias,
    )
    grads = lax.all_to_all(grads, everyone, 0, 0, tiled=True, axis_index_groups=wide)
    grads = pl.pallas_call(
        place_kernel,
        out_shape=pltpu.HBM((peers, chunk, part), BF16),
        in_specs=[vmem],
        out_specs=hbm,
        scratch_shapes=[pltpu.SemaphoreType.DMA((2,))],
        compiler_params=params,
        name="place",
    )(grads)
    return (nll.reshape(2), grads.reshape(shard_rows, part))


def solution(mesh):
    blocks = 16
    devices = mesh.devices
    split = Mesh(
        devices.reshape(blocks, devices.shape[0] // blocks, devices.shape[1]),
        ("blk", "j", "chan"),
    )
    time = ("blk", "j")
    return jax.shard_map(
        local,
        mesh=split,
        in_specs=(
            P(time, "chan"),
            P(time, "chan"),
            P(),
            P(),
            P(),
            P(),
            P(),
            P(),
            P(),
            P(),
            P(time),
            P(time),
            P(),
        ),
        out_specs=(P(("blk", "j", "chan")), P(time, "chan")),
        check_vma=False,
    )
```

```python
import jax
import jax.numpy as jnp
from jax import lax
from jax.experimental import pallas as pl
from jax.experimental.pallas import tpu as pltpu
from jax.sharding import Mesh
from jax.sharding import PartitionSpec as P

WLEN = 128
FIRST_DILATION = 8192
F32 = jnp.float32
BF16 = jnp.bfloat16
FIRST = 26


def dot(a, b):
    return jnp.dot(a, b, preferred_element_type=F32)


def dot_t(a, b):
    return lax.dot_general(a, b, (((1,), (1,)), ((), ())), preferred_element_type=F32)


def split(v):
    high = v.astype(BF16)
    return high, (v - high.astype(F32)).astype(BF16)


def fine_dot(a, b, product):
    high, low = split(a)
    rows = a.shape[0]
    both = product(jnp.concatenate([high, low], axis=0), b[0])
    return both[:rows] + both[rows:] + product(high, b[1])


def sigmoid(v):
    return 0.5 * jnp.tanh(0.5 * v) + 0.5


def position(blocks, chunk, chans):
    chan_at = lax.axis_index("chan")
    block_at = lax.axis_index("blk")
    shard_base = lax.axis_index("j") * (blocks * chans * chunk)
    base = shard_base + (chan_at * blocks + block_at) * chunk
    return base, chan_at, block_at, shard_base


def row_keep(limit, base, blocks, chunk, width):
    rows = lax.broadcasted_iota(jnp.int32, (blocks * chunk, width), 0)
    position = (rows // chunk) * FIRST_DILATION + rows % chunk + base
    return position < limit


def start_all(copies):
    for copy in copies:
        copy.start()


def wait_all(copies):
    for copy in copies:
        copy.wait()


def turn(peers):
    lead = peers - FIRST
    return [(FIRST, 0, lead), (0, lead, FIRST)]


def join_kernel(limit_ref, signal_ref, skip_ref, both_ref, limit_hbm, hold_ref, sems):
    hold_ref[0] = limit_ref[0]
    hand = pltpu.make_async_copy(hold_ref, limit_hbm, sems.at[4])
    hand.start()
    copies = []
    for source, target, size in turn(both_ref.shape[0]):
        for part, ref in enumerate((signal_ref, skip_ref)):
            copies.append(
                pltpu.make_async_copy(
                    ref.at[pl.ds(source, size)],
                    both_ref.at[pl.ds(target, size), part],
                    sems.at[len(copies)],
                )
            )
    start_all(copies)
    wait_all(copies + [hand])


def place_kernel(received_ref, grad_hbm, sems):
    copies = []
    for target, source, size in turn(received_ref.shape[0]):
        copies.append(
            pltpu.make_async_copy(
                received_ref.at[pl.ds(source, size)],
                grad_hbm.at[pl.ds(target, size)],
                sems.at[len(copies)],
            )
        )
    start_all(copies)
    wait_all(copies)


def spans(start, size, total):
    start = (start - FIRST) % total
    head = min(size, total - start)
    return [(start, head)] + ([(0, size - head)] if head < size else [])


def read_turned(ref, start, size, part):
    pieces = [
        ref[at : at + count, part].reshape(count * ref.shape[2], ref.shape[3])
        for at, count in spans(start, size, ref.shape[0])
    ]
    return pieces[0] if len(pieces) == 1 else jnp.concatenate(pieces, axis=0)


def forward_kernel(
    blocks,
    chunk,
    limit_hbm,
    bin_hbm,
    seen_hbm,
    both_ref,
    tap_ref,
    bias_ref,
    res_ref,
    skipw_hbm,
    act_hbm,
    slope_hbm,
    pool_ref,
    limit_ref,
    bin_ref,
    seen_ref,
    skipw_ref,
    act_ref,
    slope_ref,
    in_sems,
    out_sems,
):
    layers = tap_ref.shape[0]
    part = both_ref.shape[3]
    width = 2 * part
    rows = blocks * chunk
    base, chan_at, _, _ = position(blocks, chunk, 2)
    scalars = [
        pltpu.make_async_copy(limit_hbm, limit_ref, in_sems.at[0]),
        pltpu.make_async_copy(bin_hbm, bin_ref, in_sems.at[1]),
        pltpu.make_async_copy(seen_hbm, seen_ref, in_sems.at[2]),
    ]
    skipw_copy = pltpu.make_async_copy(skipw_hbm, skipw_ref, in_sems.at[3])
    skipw_copy.start()
    start_all(scalars)
    outs = []
    gated_all = []
    current, skip_sum = (
        jnp.concatenate(
            [read_turned(both_ref, c * blocks, blocks, part_at) for c in range(2)], axis=1
        )
        for part_at in range(2)
    )
    skip_sum = skip_sum.astype(F32)
    for layer in range(layers):
        late = chunk * 2**layer
        delayed = jnp.concatenate(
            [jnp.zeros((late, width), BF16), current[: rows - late]], axis=0
        )
        preact = (
            dot(delayed, tap_ref[layer, 0])
            + dot(current, tap_ref[layer, 1])
            + bias_ref[layer : layer + 1, :]
        )
        filters = jnp.tanh(preact[:, :width])
        gates = sigmoid(preact[:, width:])
        product = filters * gates
        gated = product.astype(BF16)
        gated_all.append(gated)
        if layer < layers - 1:
            current = (current.astype(F32) + dot(gated, res_ref[layer])).astype(BF16)
        act_ref[layer, :, :width] = (gates - product * filters).astype(BF16)
        act_ref[layer, :, width:] = (product - product * gates).astype(BF16)
        outs.append(
            pltpu.make_async_copy(act_ref.at[layer], act_hbm.at[layer], out_sems.at[layer])
        )
        outs[-1].start()
        if layer == 1:
            skipw_copy.wait()
        if layer > 0:
            skip_sum = skip_sum + dot(gated_all[layer - 1], skipw_ref[layer - 1])
    skip_sum = skip_sum + dot(gated_all[layers - 1], skipw_ref[layers - 1])
    wait_all(scalars)
    limit = limit_ref[0]
    keep = row_keep(limit, base, blocks, chunk, width)
    sig = sigmoid(skip_sum)
    slope = sig * (1.0 + skip_sum * (1.0 - sig))
    slope_ref[...] = jnp.where(keep, slope, 0.0).astype(BF16)
    outs.append(pltpu.make_async_copy(slope_ref, slope_hbm, out_sems.at[layers]))
    outs[-1].start()
    active = jnp.where(keep, skip_sum * sig, 0.0)
    sums = active.reshape(blocks, chunk, width).sum(axis=1)
    first = 2 * chan_at
    line = lax.broadcasted_iota(jnp.int32, (8, width), 0)
    bins = [ref[first + i].astype(F32) for ref in (bin_ref, seen_ref) for i in (0, 1)]
    extra = jnp.where(
        line == 0,
        bins[0],
        jnp.where(line == 1, bins[1], jnp.where(line == 2, bins[2], bins[3])),
    )
    sums = sums.astype(BF16)
    extra = extra.astype(BF16)
    for other in range(blocks):
        pool_ref[other, :blocks, :] = sums
        pool_ref[other, blocks:, :] = extra
    wait_all(outs)


def mixture(params, log_time, seen, mixes):
    lanes = params.shape[1]
    lane = lax.broadcasted_iota(jnp.int32, params.shape, 1)
    valid = lane < mixes
    bend_logit = jnp.tanh(params)
    log_scale = jnp.tanh(pltpu.roll(params, lanes - mixes, 1))
    bend_shape = jnp.tanh(pltpu.roll(params, lanes - 2 * mixes, 1))
    logits = 4.0 * bend_logit
    raised = jnp.where(valid, jnp.exp(logits), 0.0)
    total = jnp.sum(raised, axis=1, keepdims=True)
    log_weight = logits - jnp.log(total)
    log_shape = 0.5 * bend_shape
    shape = jnp.exp(log_shape)
    ratio = log_time - log_scale
    power = jnp.exp(shape * ratio)
    density = log_shape - log_scale + (shape - 1.0) * ratio - power
    component = jnp.where(seen, density, -power)
    likely = jnp.where(valid, jnp.exp(log_weight + component), 0.0)
    mass = jnp.sum(likely, axis=1, keepdims=True)
    nll = -jnp.log(mass)
    owned = likely / mass
    to_logit = (raised / total - owned) * 4.0 * (1.0 - bend_logit * bend_logit)
    steep = power * shape
    to_scale = jnp.where(seen, steep - shape, steep)
    to_shape = jnp.where(seen, 1.0 + shape * ratio, 0.0) - steep * ratio
    to_scale = -owned * to_scale * (1.0 - log_scale * log_scale)
    to_shape = -owned * to_shape * 0.5 * (1.0 - bend_shape * bend_shape)
    zero = jnp.zeros_like(params)
    grad = (
        jnp.where(valid, to_logit, zero)
        + pltpu.roll(jnp.where(valid, to_scale, zero), mixes, 1)
        + pltpu.roll(jnp.where(valid, to_shape, zero), 2 * mixes, 1)
    )
    return nll, grad


def backward_kernel(
    blocks,
    chunk,
    limit_hbm,
    pool_ref,
    act_hbm,
    slope_hbm,
    skipw_hbm,
    tap_ref,
    res_ref,
    head1_ref,
    headb1_ref,
    head2_ref,
    headb2_ref,
    nll_ref,
    grad_ref,
    limit_ref,
    act_ref,
    slope_ref,
    skipw_ref,
    pad_ref,
    bias2_ref,
    sems,
):
    layers = tap_ref.shape[0]
    width = slope_ref.shape[1]
    limit_copy = pltpu.make_async_copy(limit_hbm, limit_ref, sems.at[0])
    copies = [
        pltpu.make_async_copy(slope_hbm, slope_ref, sems.at[1]),
        pltpu.make_async_copy(skipw_hbm, skipw_ref, sems.at[2]),
        pltpu.make_async_copy(act_hbm, act_ref, sems.at[3]),
    ]
    limit_copy.start()
    start_all(copies)
    part = width // 2
    rows = blocks * chunk
    lanes = pad_ref.shape[0]
    outs = head2_ref.shape[0]
    base, chan_at, block_at, shard_base = position(blocks, chunk, 2)
    half = blocks // 2
    received = pool_ref[...].astype(F32)
    first = FIRST % blocks
    received = jnp.concatenate([received[blocks - first :], received[: blocks - first]], axis=0)
    sums = jnp.concatenate(
        [
            received[:half, :blocks, :].sum(axis=0),
            received[half:, :blocks, :].sum(axis=0),
        ],
        axis=0,
    )
    bins = jnp.concatenate([received[:, blocks, :lanes], received[:, blocks + 1, :lanes]], axis=0)
    seen = (
        jnp.concatenate(
            [received[:, blocks + 2, :lanes], received[:, blocks + 3, :lanes]], axis=0
        )
        == 1.0
    )
    log_time = jnp.log((bins + 1.0) / 8.0)
    window = lax.broadcasted_iota(jnp.int32, (2 * blocks, width), 0)
    start = (
        (window % blocks) * FIRST_DILATION
        + shard_base
        + (2 * chan_at + window // blocks) * WLEN
    )
    limit_copy.wait()
    limit = limit_ref[0]
    count = jnp.clip(limit - start, 1, WLEN).astype(F32)
    pooled = sums / count
    pad_ref[...] = jnp.zeros_like(pad_ref)
    pad_ref[:outs, :] = head2_ref[...]
    head1 = split(head1_ref[...])
    head2 = split(pad_ref[...])
    bias2_ref[...] = jnp.zeros_like(bias2_ref)
    bias2_ref[:, :outs] = headb2_ref[...]
    inner = fine_dot(pooled, head1, dot) + headb1_ref[...]
    open_inner = sigmoid(inner)
    hidden = inner * open_inner
    params = fine_dot(hidden, head2, dot_t) + bias2_ref[...]
    nll, to_params = mixture(params, log_time, seen, outs // 3)
    to_hidden = fine_dot(to_params, head2, dot)
    to_inner = to_hidden * open_inner * (1.0 + inner * (1.0 - open_inner))
    to_pooled = fine_dot(to_inner, head1, dot_t)

    row = lax.broadcasted_iota(jnp.int32, (2 * blocks, 2), 0)
    col = lax.broadcasted_iota(jnp.int32, (2 * blocks, 2), 1)
    mine = row == col * blocks + block_at
    nll_ref[...] = jnp.sum(jnp.where(mine, nll, 0.0), axis=0, keepdims=True)

    own_pool = jnp.where(block_at < half, to_pooled[:blocks], to_pooled[blocks:])
    spread = jnp.broadcast_to(own_pool[:, None, :], (blocks, chunk, width)).reshape(rows, width)
    wait_all(copies)
    grad_skip = (spread * slope_ref[...].astype(F32)).astype(BF16)
    grad_rows = None
    for layer in range(layers - 1, -1, -1):
        early = chunk * 2**layer
        grad_gated = dot_t(grad_skip, skipw_ref[layer])
        if grad_rows is not None:
            grad_gated = grad_gated + dot_t(grad_rows, res_ref[layer])
        twice = jnp.concatenate([grad_gated, grad_gated], axis=1)
        preact_grad = (twice * act_ref[layer].astype(F32)).astype(BF16)
        ahead = jnp.concatenate(
            [preact_grad[early:], jnp.zeros((early, 2 * width), BF16)], axis=0
        )
        summed = dot_t(preact_grad, tap_ref[layer, 1]) + dot_t(ahead, tap_ref[layer, 0])
        if grad_rows is not None:
            summed = summed + grad_rows.astype(F32)
        grad_rows = summed.astype(BF16)
    peers = grad_ref.shape[0]
    for c in range(2):
        done = 0
        for at, count in spans(c * blocks, blocks, peers):
            piece = grad_rows[done * chunk : (done + count) * chunk, c * part : (c + 1) * part]
            grad_ref[at : at + count] = piece.reshape(count, chunk, part)
            done += count


def local(
    signal,
    skip_in,
    tap_weight,
    tap_bias,
    res_weight,
    skip_weight,
    head_w1,
    head_b1,
    head_w2,
    head_second_bias,
    event_bin,
    observed,
    valid_len,
):
    blocks = lax.axis_size("blk")
    chans = lax.axis_size("chan")
    shard_rows, part = signal.shape
    width = part * chans
    peers = blocks * chans
    chunk = shard_rows // peers
    rows = blocks * chunk
    layers = tap_weight.shape[0]
    shape = jax.ShapeDtypeStruct
    smem = pl.BlockSpec(memory_space=pltpu.SMEM)
    vmem = pl.BlockSpec(memory_space=pltpu.VMEM)
    hbm = pl.BlockSpec(memory_space=pltpu.HBM)
    params = pltpu.CompilerParams(vmem_limit_bytes=24 << 20)

    def stay(array):
        return pltpu.with_memory_space_constraint(array, pltpu.HBM)


    both, limit = pl.pallas_call(
        join_kernel,
        out_shape=(shape((peers, 2, chunk, part), BF16), pltpu.HBM((8,), jnp.int32)),
        in_specs=[smem, hbm, hbm],
        out_specs=(vmem, hbm),
        scratch_shapes=[pltpu.SMEM((8,), jnp.int32), pltpu.SemaphoreType.DMA((5,))],
        compiler_params=params,
        cost_estimate=pl.CostEstimate(
            flops=40_000_000_000, bytes_accessed=2 * peers * chunk * part * 4, transcendentals=0
        ),
        name="join",
    )(valid_len, stay(signal.reshape(peers, chunk, part)), stay(skip_in.reshape(peers, chunk, part)))
    shards = lax.axis_size("j")
    everyone = ("blk", "j", "chan")
    order = [(FIRST + i) % peers for i in range(peers)]
    wide = [
        [((k % blocks) * shards + j) * chans + k // blocks for k in order] for j in range(shards)
    ]
    first = FIRST % blocks
    near = [[(first + i) % blocks for i in range(blocks)]]
    both = lax.all_to_all(both, everyone, 0, 0, tiled=True, axis_index_groups=wide)

    acts, slope, pool = pl.pallas_call(
        lambda *refs: forward_kernel(blocks, chunk, *refs),
        out_shape=(
            pltpu.HBM((layers, rows, 2 * width), BF16),
            pltpu.HBM((rows, width), BF16),
            shape((blocks, blocks + 8, width), BF16),
        ),
        in_specs=[hbm] * 3 + [vmem] * 4 + [hbm],
        out_specs=(hbm, hbm, vmem),
        scratch_shapes=[
            pltpu.SMEM((8,), jnp.int32),
            pltpu.SMEM(event_bin.shape, jnp.int32),
            pltpu.SMEM(observed.shape, jnp.int32),
            pltpu.VMEM(skip_weight.shape, BF16),
            pltpu.VMEM((layers, rows, 2 * width), BF16),
            pltpu.VMEM((rows, width), BF16),
            pltpu.SemaphoreType.DMA((4,)),
            pltpu.SemaphoreType.DMA((layers + 1,)),
        ],
        compiler_params=params,
        cost_estimate=pl.CostEstimate(
            flops=40_000_000_000, bytes_accessed=8 << 20, transcendentals=0
        ),
        name="forward",
    )(
        stay(limit),
        stay(event_bin),
        stay(observed),
        both,
        tap_weight,
        tap_bias,
        res_weight,
        stay(skip_weight),
    )

    pool = lax.all_to_all(pool, "blk", 0, 0, tiled=True, axis_index_groups=near)

    head_b1 = head_b1.reshape(1, -1)
    head_second_bias = head_second_bias.reshape(1, -1)
    nll, grads = pl.pallas_call(
        lambda *refs: backward_kernel(blocks, chunk, *refs),
        out_shape=(
            shape((1, 2), F32),
            shape((peers, chunk, part), BF16),
        ),
        in_specs=[hbm, vmem] + [hbm] * 3 + [vmem] * 6,
        out_specs=(vmem, vmem),
        scratch_shapes=[
            pltpu.SMEM((8,), jnp.int32),
            pltpu.VMEM((layers, rows, 2 * width), BF16),
            pltpu.VMEM((rows, width), BF16),
            pltpu.VMEM(skip_weight.shape, BF16),
            pltpu.VMEM((128, width), F32),
            pltpu.VMEM((1, 128), F32),
            pltpu.SemaphoreType.DMA((4,)),
        ],
        compiler_params=params,
        name="backward",
    )(
        stay(limit),
        pool,
        stay(acts),
        stay(slope),
        stay(skip_weight),
        tap_weight,
        res_weight,
        head_w1,
        head_b1,
        head_w2.T,
        head_second_bias,
    )
    grads = lax.all_to_all(grads, everyone, 0, 0, tiled=True, axis_index_groups=wide)
    grads = pl.pallas_call(
        place_kernel,
        out_shape=pltpu.HBM((peers, chunk, part), BF16),
        in_specs=[vmem],
        out_specs=hbm,
        scratch_shapes=[pltpu.SemaphoreType.DMA((2,))],
        compiler_params=params,
        name="place",
    )(grads)
    return (nll.reshape(2), grads.reshape(shard_rows, part))


def solution(mesh):
    blocks = 16
    devices = mesh.devices
    split = Mesh(
        devices.reshape(blocks, devices.shape[0] // blocks, devices.shape[1]),
        ("blk", "j", "chan"),
    )
    time = ("blk", "j")
    return jax.shard_map(
        local,
        mesh=split,
        in_specs=(
            P(time, "chan"),
            P(time, "chan"),
            P(),
            P(),
            P(),
            P(),
            P(),
            P(),
            P(),
            P(),
            P(time),
            P(time),
            P(),
        ),
        out_specs=(P(("blk", "j", "chan")), P(time, "chan")),
        check_vma=False,
    )
```

```python
import jax
import jax.numpy as jnp
from jax import lax
from jax.experimental import pallas as pl
from jax.experimental.pallas import tpu as pltpu
from jax.sharding import Mesh
from jax.sharding import PartitionSpec as P

WLEN = 128
FIRST_DILATION = 8192
F32 = jnp.float32
BF16 = jnp.bfloat16
FIRST = 26


def dot(a, b):
    return jnp.dot(a, b, preferred_element_type=F32)


def dot_t(a, b):
    return lax.dot_general(a, b, (((1,), (1,)), ((), ())), preferred_element_type=F32)


def split(v):
    high = v.astype(BF16)
    return high, (v - high.astype(F32)).astype(BF16)


def fine_dot(a, b, product):
    high, low = split(a)
    rows = a.shape[0]
    both = product(jnp.concatenate([high, low], axis=0), b[0])
    return both[:rows] + both[rows:] + product(high, b[1])


def sigmoid(v):
    return 0.5 * jnp.tanh(0.5 * v) + 0.5


def position(blocks, chunk, chans):
    chan_at = lax.axis_index("chan")
    block_at = lax.axis_index("blk")
    shard_base = lax.axis_index("j") * (blocks * chans * chunk)
    base = shard_base + (chan_at * blocks + block_at) * chunk
    return base, chan_at, block_at, shard_base


def row_keep(limit, base, blocks, chunk, width):
    rows = lax.broadcasted_iota(jnp.int32, (blocks * chunk, width), 0)
    position = (rows // chunk) * FIRST_DILATION + rows % chunk + base
    return position < limit


def start_all(copies):
    for copy in copies:
        copy.start()


def wait_all(copies):
    for copy in copies:
        copy.wait()


def turn(peers):
    lead = peers - FIRST
    return [(FIRST, 0, lead), (0, lead, FIRST)]


def join_kernel(limit_ref, signal_ref, skip_ref, both_ref, limit_hbm, hold_ref, sems):
    hold_ref[0] = limit_ref[0]
    hand = pltpu.make_async_copy(hold_ref, limit_hbm, sems.at[4])
    hand.start()
    copies = []
    for source, target, size in turn(both_ref.shape[0]):
        for part, ref in enumerate((signal_ref, skip_ref)):
            copies.append(
                pltpu.make_async_copy(
                    ref.at[pl.ds(source, size)],
                    both_ref.at[pl.ds(target, size), part],
                    sems.at[len(copies)],
                )
            )
    start_all(copies)
    wait_all(copies + [hand])


def place_kernel(received_ref, grad_hbm, sems):
    copies = []
    for target, source, size in turn(received_ref.shape[0]):
        copies.append(
            pltpu.make_async_copy(
                received_ref.at[pl.ds(source, size)],
                grad_hbm.at[pl.ds(target, size)],
                sems.at[len(copies)],
            )
        )
    start_all(copies)
    wait_all(copies)


def spans(start, size, total):
    start = (start - FIRST) % total
    head = min(size, total - start)
    return [(start, head)] + ([(0, size - head)] if head < size else [])


def read_turned(ref, start, size, part):
    pieces = [
        ref[at : at + count, part].reshape(count * ref.shape[2], ref.shape[3])
        for at, count in spans(start, size, ref.shape[0])
    ]
    return pieces[0] if len(pieces) == 1 else jnp.concatenate(pieces, axis=0)


def forward_kernel(
    blocks,
    chunk,
    limit_hbm,
    bin_hbm,
    seen_hbm,
    both_ref,
    tap_ref,
    bias_ref,
    res_ref,
    skipw_hbm,
    act_hbm,
    slope_ref,
    pool_ref,
    limit_ref,
    bin_ref,
    seen_ref,
    skipw_ref,
    act_ref,
    in_sems,
    out_sems,
):
    layers = tap_ref.shape[0]
    part = both_ref.shape[3]
    width = 2 * part
    rows = blocks * chunk
    base, chan_at, _, _ = position(blocks, chunk, 2)
    scalars = [
        pltpu.make_async_copy(limit_hbm, limit_ref, in_sems.at[0]),
        pltpu.make_async_copy(bin_hbm, bin_ref, in_sems.at[1]),
        pltpu.make_async_copy(seen_hbm, seen_ref, in_sems.at[2]),
    ]
    skipw_copy = pltpu.make_async_copy(skipw_hbm, skipw_ref, in_sems.at[3])
    skipw_copy.start()
    start_all(scalars)
    outs = []
    gated_all = []
    current, skip_sum = (
        jnp.concatenate(
            [read_turned(both_ref, c * blocks, blocks, part_at) for c in range(2)], axis=1
        )
        for part_at in range(2)
    )
    skip_sum = skip_sum.astype(F32)
    for layer in range(layers):
        late = chunk * 2**layer
        delayed = jnp.concatenate(
            [jnp.zeros((late, width), BF16), current[: rows - late]], axis=0
        )
        preact = (
            dot(delayed, tap_ref[layer, 0])
            + dot(current, tap_ref[layer, 1])
            + bias_ref[layer : layer + 1, :]
        )
        filters = jnp.tanh(preact[:, :width])
        gates = sigmoid(preact[:, width:])
        product = filters * gates
        gated = product.astype(BF16)
        gated_all.append(gated)
        if layer < layers - 1:
            current = (current.astype(F32) + dot(gated, res_ref[layer])).astype(BF16)
        act_ref[layer, :, :width] = (gates - product * filters).astype(BF16)
        act_ref[layer, :, width:] = (product - product * gates).astype(BF16)
        outs.append(
            pltpu.make_async_copy(act_ref.at[layer], act_hbm.at[layer], out_sems.at[layer])
        )
        outs[-1].start()
        if layer == 1:
            skipw_copy.wait()
        if layer > 0:
            skip_sum = skip_sum + dot(gated_all[layer - 1], skipw_ref[layer - 1])
    skip_sum = skip_sum + dot(gated_all[layers - 1], skipw_ref[layers - 1])
    wait_all(scalars)
    limit = limit_ref[0]
    keep = row_keep(limit, base, blocks, chunk, width)
    sig = sigmoid(skip_sum)
    slope = sig * (1.0 + skip_sum * (1.0 - sig))
    slope_ref[...] = jnp.where(keep, slope, 0.0).astype(BF16)
    active = jnp.where(keep, skip_sum * sig, 0.0)
    sums = active.reshape(blocks, chunk, width).sum(axis=1)
    first = 2 * chan_at
    line = lax.broadcasted_iota(jnp.int32, (8, width), 0)
    bins = [ref[first + i].astype(F32) for ref in (bin_ref, seen_ref) for i in (0, 1)]
    extra = jnp.where(
        line == 0,
        bins[0],
        jnp.where(line == 1, bins[1], jnp.where(line == 2, bins[2], bins[3])),
    )
    sums = sums.astype(BF16)
    extra = extra.astype(BF16)
    for other in range(blocks):
        pool_ref[other, :blocks, :] = sums
        pool_ref[other, blocks:, :] = extra
    wait_all(outs)


def mixture(params, log_time, seen, mixes):
    lanes = params.shape[1]
    lane = lax.broadcasted_iota(jnp.int32, params.shape, 1)
    valid = lane < mixes
    bend_logit = jnp.tanh(params)
    log_scale = jnp.tanh(pltpu.roll(params, lanes - mixes, 1))
    bend_shape = jnp.tanh(pltpu.roll(params, lanes - 2 * mixes, 1))
    logits = 4.0 * bend_logit
    raised = jnp.where(valid, jnp.exp(logits), 0.0)
    total = jnp.sum(raised, axis=1, keepdims=True)
    log_weight = logits - jnp.log(total)
    log_shape = 0.5 * bend_shape
    shape = jnp.exp(log_shape)
    ratio = log_time - log_scale
    power = jnp.exp(shape * ratio)
    density = log_shape - log_scale + (shape - 1.0) * ratio - power
    component = jnp.where(seen, density, -power)
    likely = jnp.where(valid, jnp.exp(log_weight + component), 0.0)
    mass = jnp.sum(likely, axis=1, keepdims=True)
    nll = -jnp.log(mass)
    owned = likely / mass
    to_logit = (raised / total - owned) * 4.0 * (1.0 - bend_logit * bend_logit)
    steep = power * shape
    to_scale = jnp.where(seen, steep - shape, steep)
    to_shape = jnp.where(seen, 1.0 + shape * ratio, 0.0) - steep * ratio
    to_scale = -owned * to_scale * (1.0 - log_scale * log_scale)
    to_shape = -owned * to_shape * 0.5 * (1.0 - bend_shape * bend_shape)
    zero = jnp.zeros_like(params)
    grad = (
        jnp.where(valid, to_logit, zero)
        + pltpu.roll(jnp.where(valid, to_scale, zero), mixes, 1)
        + pltpu.roll(jnp.where(valid, to_shape, zero), 2 * mixes, 1)
    )
    return nll, grad


def backward_kernel(
    blocks,
    chunk,
    limit_hbm,
    pool_ref,
    act_hbm,
    slope_ref,
    skipw_hbm,
    tap_ref,
    res_ref,
    head1_ref,
    headb1_ref,
    head2_ref,
    headb2_ref,
    nll_ref,
    grad_ref,
    limit_ref,
    act_ref,
    skipw_ref,
    pad_ref,
    bias2_ref,
    sems,
):
    layers = tap_ref.shape[0]
    width = slope_ref.shape[1]
    limit_copy = pltpu.make_async_copy(limit_hbm, limit_ref, sems.at[0])
    copies = [
        pltpu.make_async_copy(skipw_hbm, skipw_ref, sems.at[1]),
        pltpu.make_async_copy(act_hbm, act_ref, sems.at[2]),
    ]
    limit_copy.start()
    start_all(copies)
    part = width // 2
    rows = blocks * chunk
    lanes = pad_ref.shape[0]
    outs = head2_ref.shape[0]
    base, chan_at, block_at, shard_base = position(blocks, chunk, 2)
    half = blocks // 2
    received = pool_ref[...].astype(F32)
    first = FIRST % blocks
    received = jnp.concatenate([received[blocks - first :], received[: blocks - first]], axis=0)
    sums = jnp.concatenate(
        [
            received[:half, :blocks, :].sum(axis=0),
            received[half:, :blocks, :].sum(axis=0),
        ],
        axis=0,
    )
    bins = jnp.concatenate([received[:, blocks, :lanes], received[:, blocks + 1, :lanes]], axis=0)
    seen = (
        jnp.concatenate(
            [received[:, blocks + 2, :lanes], received[:, blocks + 3, :lanes]], axis=0
        )
        == 1.0
    )
    log_time = jnp.log((bins + 1.0) / 8.0)
    window = lax.broadcasted_iota(jnp.int32, (2 * blocks, width), 0)
    start = (
        (window % blocks) * FIRST_DILATION
        + shard_base
        + (2 * chan_at + window // blocks) * WLEN
    )
    limit_copy.wait()
    limit = limit_ref[0]
    count = jnp.clip(limit - start, 1, WLEN).astype(F32)
    pooled = sums / count
    pad_ref[...] = jnp.zeros_like(pad_ref)
    pad_ref[:outs, :] = head2_ref[...]
    head1 = split(head1_ref[...])
    head2 = split(pad_ref[...])
    bias2_ref[...] = jnp.zeros_like(bias2_ref)
    bias2_ref[:, :outs] = headb2_ref[...]
    inner = fine_dot(pooled, head1, dot) + headb1_ref[...]
    open_inner = sigmoid(inner)
    hidden = inner * open_inner
    params = fine_dot(hidden, head2, dot_t) + bias2_ref[...]
    nll, to_params = mixture(params, log_time, seen, outs // 3)
    to_hidden = fine_dot(to_params, head2, dot)
    to_inner = to_hidden * open_inner * (1.0 + inner * (1.0 - open_inner))
    to_pooled = fine_dot(to_inner, head1, dot_t)

    row = lax.broadcasted_iota(jnp.int32, (2 * blocks, 2), 0)
    col = lax.broadcasted_iota(jnp.int32, (2 * blocks, 2), 1)
    mine = row == col * blocks + block_at
    nll_ref[...] = jnp.sum(jnp.where(mine, nll, 0.0), axis=0, keepdims=True)

    own_pool = jnp.where(block_at < half, to_pooled[:blocks], to_pooled[blocks:])
    spread = jnp.broadcast_to(own_pool[:, None, :], (blocks, chunk, width)).reshape(rows, width)
    wait_all(copies)
    grad_skip = (spread * slope_ref[...].astype(F32)).astype(BF16)
    grad_rows = None
    for layer in range(layers - 1, -1, -1):
        early = chunk * 2**layer
        grad_gated = dot_t(grad_skip, skipw_ref[layer])
        if grad_rows is not None:
            grad_gated = grad_gated + dot_t(grad_rows, res_ref[layer])
        twice = jnp.concatenate([grad_gated, grad_gated], axis=1)
        preact_grad = (twice * act_ref[layer].astype(F32)).astype(BF16)
        ahead = jnp.concatenate(
            [preact_grad[early:], jnp.zeros((early, 2 * width), BF16)], axis=0
        )
        summed = dot_t(preact_grad, tap_ref[layer, 1]) + dot_t(ahead, tap_ref[layer, 0])
        if grad_rows is not None:
            summed = summed + grad_rows.astype(F32)
        grad_rows = summed.astype(BF16)
    peers = grad_ref.shape[0]
    for c in range(2):
        done = 0
        for at, count in spans(c * blocks, blocks, peers):
            piece = grad_rows[done * chunk : (done + count) * chunk, c * part : (c + 1) * part]
            grad_ref[at : at + count] = piece.reshape(count, chunk, part)
            done += count


def local(
    signal,
    skip_in,
    tap_weight,
    tap_bias,
    res_weight,
    skip_weight,
    head_w1,
    head_b1,
    head_w2,
    head_second_bias,
    event_bin,
    observed,
    valid_len,
):
    blocks = lax.axis_size("blk")
    chans = lax.axis_size("chan")
    shard_rows, part = signal.shape
    width = part * chans
    peers = blocks * chans
    chunk = shard_rows // peers
    rows = blocks * chunk
    layers = tap_weight.shape[0]
    shape = jax.ShapeDtypeStruct
    smem = pl.BlockSpec(memory_space=pltpu.SMEM)
    vmem = pl.BlockSpec(memory_space=pltpu.VMEM)
    hbm = pl.BlockSpec(memory_space=pltpu.HBM)
    params = pltpu.CompilerParams(vmem_limit_bytes=24 << 20)

    def stay(array):
        return pltpu.with_memory_space_constraint(array, pltpu.HBM)


    both, limit = pl.pallas_call(
        join_kernel,
        out_shape=(shape((peers, 2, chunk, part), BF16), pltpu.HBM((8,), jnp.int32)),
        in_specs=[smem, hbm, hbm],
        out_specs=(vmem, hbm),
        scratch_shapes=[pltpu.SMEM((8,), jnp.int32), pltpu.SemaphoreType.DMA((5,))],
        compiler_params=params,
        cost_estimate=pl.CostEstimate(
            flops=40_000_000_000, bytes_accessed=2 * peers * chunk * part * 4, transcendentals=0
        ),
        name="join",
    )(valid_len, stay(signal.reshape(peers, chunk, part)), stay(skip_in.reshape(peers, chunk, part)))
    shards = lax.axis_size("j")
    everyone = ("blk", "j", "chan")
    order = [(FIRST + i) % peers for i in range(peers)]
    wide = [
        [((k % blocks) * shards + j) * chans + k // blocks for k in order] for j in range(shards)
    ]
    first = FIRST % blocks
    near = [[(first + i) % blocks for i in range(blocks)]]
    both = lax.all_to_all(both, everyone, 0, 0, tiled=True, axis_index_groups=wide)

    acts, slope, pool = pl.pallas_call(
        lambda *refs: forward_kernel(blocks, chunk, *refs),
        out_shape=(
            pltpu.HBM((layers, rows, 2 * width), BF16),
            shape((rows, width), BF16),
            shape((blocks, blocks + 8, width), BF16),
        ),
        in_specs=[hbm] * 3 + [vmem] * 4 + [hbm],
        out_specs=(hbm, vmem, vmem),
        scratch_shapes=[
            pltpu.SMEM((8,), jnp.int32),
            pltpu.SMEM(event_bin.shape, jnp.int32),
            pltpu.SMEM(observed.shape, jnp.int32),
            pltpu.VMEM(skip_weight.shape, BF16),
            pltpu.VMEM((layers, rows, 2 * width), BF16),
            pltpu.SemaphoreType.DMA((4,)),
            pltpu.SemaphoreType.DMA((layers,)),
        ],
        compiler_params=params,
        cost_estimate=pl.CostEstimate(
            flops=40_000_000_000, bytes_accessed=8 << 20, transcendentals=0
        ),
        name="forward",
    )(
        stay(limit),
        stay(event_bin),
        stay(observed),
        both,
        tap_weight,
        tap_bias,
        res_weight,
        stay(skip_weight),
    )

    pool = lax.all_to_all(pool, "blk", 0, 0, tiled=True, axis_index_groups=near)

    head_b1 = head_b1.reshape(1, -1)
    head_second_bias = head_second_bias.reshape(1, -1)
    nll, grads = pl.pallas_call(
        lambda *refs: backward_kernel(blocks, chunk, *refs),
        out_shape=(
            shape((1, 2), F32),
            shape((peers, chunk, part), BF16),
        ),
        in_specs=[hbm, vmem, hbm, vmem, hbm] + [vmem] * 6,
        out_specs=(vmem, vmem),
        scratch_shapes=[
            pltpu.SMEM((8,), jnp.int32),
            pltpu.VMEM((layers, rows, 2 * width), BF16),
            pltpu.VMEM(skip_weight.shape, BF16),
            pltpu.VMEM((128, width), F32),
            pltpu.VMEM((1, 128), F32),
            pltpu.SemaphoreType.DMA((3,)),
        ],
        compiler_params=params,
        name="backward",
    )(
        stay(limit),
        pool,
        stay(acts),
        slope,
        stay(skip_weight),
        tap_weight,
        res_weight,
        head_w1,
        head_b1,
        head_w2.T,
        head_second_bias,
    )
    grads = lax.all_to_all(grads, everyone, 0, 0, tiled=True, axis_index_groups=wide)
    grads = pl.pallas_call(
        place_kernel,
        out_shape=pltpu.HBM((peers, chunk, part), BF16),
        in_specs=[vmem],
        out_specs=hbm,
        scratch_shapes=[pltpu.SemaphoreType.DMA((2,))],
        compiler_params=params,
        name="place",
    )(grads)
    return (nll.reshape(2), grads.reshape(shard_rows, part))


def solution(mesh):
    blocks = 16
    devices = mesh.devices
    split = Mesh(
        devices.reshape(blocks, devices.shape[0] // blocks, devices.shape[1]),
        ("blk", "j", "chan"),
    )
    time = ("blk", "j")
    return jax.shard_map(
        local,
        mesh=split,
        in_specs=(
            P(time, "chan"),
            P(time, "chan"),
            P(),
            P(),
            P(),
            P(),
            P(),
            P(),
            P(),
            P(),
            P(time),
            P(time),
            P(),
        ),
        out_specs=(P(("blk", "j", "chan")), P(time, "chan")),
        check_vma=False,
    )
```

```python
import jax
import jax.numpy as jnp
from jax import lax
from jax.experimental import pallas as pl
from jax.experimental.pallas import tpu as pltpu
from jax.sharding import Mesh
from jax.sharding import PartitionSpec as P

WLEN = 128
FIRST_DILATION = 8192
F32 = jnp.float32
BF16 = jnp.bfloat16
FIRST = 10


def dot(a, b):
    return jnp.dot(a, b, preferred_element_type=F32)


def dot_t(a, b):
    return lax.dot_general(a, b, (((1,), (1,)), ((), ())), preferred_element_type=F32)


def split(v):
    high = v.astype(BF16)
    return high, (v - high.astype(F32)).astype(BF16)


def fine_dot(a, b, product):
    high, low = split(a)
    rows = a.shape[0]
    both = product(jnp.concatenate([high, low], axis=0), b[0])
    return both[:rows] + both[rows:] + product(high, b[1])


def sigmoid(v):
    return 0.5 * jnp.tanh(0.5 * v) + 0.5


def position(blocks, chunk, chans):
    chan_at = lax.axis_index("chan")
    block_at = lax.axis_index("blk")
    shard_base = lax.axis_index("j") * (blocks * chans * chunk)
    base = shard_base + (chan_at * blocks + block_at) * chunk
    return base, chan_at, block_at, shard_base


def row_keep(limit, base, blocks, chunk, width):
    rows = lax.broadcasted_iota(jnp.int32, (blocks * chunk, width), 0)
    position = (rows // chunk) * FIRST_DILATION + rows % chunk + base
    return position < limit


def start_all(copies):
    for copy in copies:
        copy.start()


def wait_all(copies):
    for copy in copies:
        copy.wait()


def spans(blocks):
    lead = blocks - FIRST
    return [(FIRST, 0, lead), (0, lead, FIRST)]


def join_kernel(limit_ref, signal_ref, skip_ref, both_ref, limit_hbm, hold_ref, sems):
    hold_ref[0] = limit_ref[0]
    copies = [pltpu.make_async_copy(hold_ref, limit_hbm, sems.at[0])]
    blocks, chans = both_ref.shape[:2]
    for c in range(chans):
        for block, at, count in spans(blocks):
            for part, ref in enumerate((signal_ref, skip_ref)):
                copies.append(
                    pltpu.make_async_copy(
                        ref.at[pl.ds(c * blocks + block, count)],
                        both_ref.at[pl.ds(at, count), chans - 1 - c, part],
                        sems.at[len(copies)],
                    )
                )
    start_all(copies)
    wait_all(copies)


def place_kernel(received_ref, grad_hbm, sems):
    copies = []
    blocks, chans = received_ref.shape[:2]
    for c in range(chans):
        for block, at, count in spans(blocks):
            copies.append(
                pltpu.make_async_copy(
                    received_ref.at[pl.ds(at, count), chans - 1 - c],
                    grad_hbm.at[pl.ds(c * blocks + block, count)],
                    sems.at[len(copies)],
                )
            )
    start_all(copies)
    wait_all(copies)


def read_turned(ref, c, part):
    blocks, chans = ref.shape[:2]
    pieces = [
        ref[at : at + count, chans - 1 - c, part].reshape(count * ref.shape[3], ref.shape[4])
        for _, at, count in sorted(spans(blocks))
    ]
    return jnp.concatenate(pieces, axis=0)


def forward_kernel(
    blocks,
    chunk,
    limit_hbm,
    bin_hbm,
    seen_hbm,
    both_ref,
    tap_ref,
    bias_ref,
    res_ref,
    skipw_hbm,
    act_hbm,
    slope_ref,
    pool_ref,
    limit_ref,
    bin_ref,
    seen_ref,
    skipw_ref,
    act_ref,
    in_sems,
    out_sems,
):
    layers = tap_ref.shape[0]
    part = both_ref.shape[4]
    width = 2 * part
    rows = blocks * chunk
    base, chan_at, _, _ = position(blocks, chunk, 2)
    scalars = [
        pltpu.make_async_copy(limit_hbm, limit_ref, in_sems.at[0]),
        pltpu.make_async_copy(bin_hbm, bin_ref, in_sems.at[1]),
        pltpu.make_async_copy(seen_hbm, seen_ref, in_sems.at[2]),
    ]
    skipw_copy = pltpu.make_async_copy(skipw_hbm, skipw_ref, in_sems.at[3])
    skipw_copy.start()
    start_all(scalars)
    outs = []
    gated_all = []
    current, skip_sum = (
        jnp.concatenate(
            [read_turned(both_ref, c, part_at) for c in range(2)], axis=1
        )
        for part_at in range(2)
    )
    skip_sum = skip_sum.astype(F32)
    for layer in range(layers):
        late = chunk * 2**layer
        delayed = jnp.concatenate(
            [jnp.zeros((late, width), BF16), current[: rows - late]], axis=0
        )
        preact = (
            dot(delayed, tap_ref[layer, 0])
            + dot(current, tap_ref[layer, 1])
            + bias_ref[layer : layer + 1, :]
        )
        filters = jnp.tanh(preact[:, :width])
        gates = sigmoid(preact[:, width:])
        product = filters * gates
        gated = product.astype(BF16)
        gated_all.append(gated)
        if layer < layers - 1:
            current = (current.astype(F32) + dot(gated, res_ref[layer])).astype(BF16)
        act_ref[layer, :, :width] = (gates - product * filters).astype(BF16)
        act_ref[layer, :, width:] = (product - product * gates).astype(BF16)
        outs.append(
            pltpu.make_async_copy(act_ref.at[layer], act_hbm.at[layer], out_sems.at[layer])
        )
        outs[-1].start()
        if layer == 1:
            skipw_copy.wait()
        if layer > 0:
            skip_sum = skip_sum + dot(gated_all[layer - 1], skipw_ref[layer - 1])
    skip_sum = skip_sum + dot(gated_all[layers - 1], skipw_ref[layers - 1])
    wait_all(scalars)
    limit = limit_ref[0]
    keep = row_keep(limit, base, blocks, chunk, width)
    sig = sigmoid(skip_sum)
    slope = sig * (1.0 + skip_sum * (1.0 - sig))
    slope_ref[...] = jnp.where(keep, slope, 0.0).astype(BF16)
    active = jnp.where(keep, skip_sum * sig, 0.0)
    sums = active.reshape(blocks, chunk, width).sum(axis=1)
    first = 2 * chan_at
    line = lax.broadcasted_iota(jnp.int32, (8, width), 0)
    bins = [ref[first + i].astype(F32) for ref in (bin_ref, seen_ref) for i in (0, 1)]
    extra = jnp.where(
        line == 0,
        bins[0],
        jnp.where(line == 1, bins[1], jnp.where(line == 2, bins[2], bins[3])),
    )
    sums = sums.astype(BF16)
    extra = extra.astype(BF16)
    for other in range(blocks):
        pool_ref[other, :blocks, :] = sums
        pool_ref[other, blocks:, :] = extra
    wait_all(outs)


def mixture(params, log_time, seen, mixes):
    lanes = params.shape[1]
    lane = lax.broadcasted_iota(jnp.int32, params.shape, 1)
    valid = lane < mixes
    bend_logit = jnp.tanh(params)
    log_scale = jnp.tanh(pltpu.roll(params, lanes - mixes, 1))
    bend_shape = jnp.tanh(pltpu.roll(params, lanes - 2 * mixes, 1))
    logits = 4.0 * bend_logit
    raised = jnp.where(valid, jnp.exp(logits), 0.0)
    total = jnp.sum(raised, axis=1, keepdims=True)
    log_weight = logits - jnp.log(total)
    log_shape = 0.5 * bend_shape
    shape = jnp.exp(log_shape)
    ratio = log_time - log_scale
    power = jnp.exp(shape * ratio)
    density = log_shape - log_scale + (shape - 1.0) * ratio - power
    component = jnp.where(seen, density, -power)
    likely = jnp.where(valid, jnp.exp(log_weight + component), 0.0)
    mass = jnp.sum(likely, axis=1, keepdims=True)
    nll = -jnp.log(mass)
    owned = likely / mass
    to_logit = (raised / total - owned) * 4.0 * (1.0 - bend_logit * bend_logit)
    steep = power * shape
    to_scale = jnp.where(seen, steep - shape, steep)
    to_shape = jnp.where(seen, 1.0 + shape * ratio, 0.0) - steep * ratio
    to_scale = -owned * to_scale * (1.0 - log_scale * log_scale)
    to_shape = -owned * to_shape * 0.5 * (1.0 - bend_shape * bend_shape)
    zero = jnp.zeros_like(params)
    grad = (
        jnp.where(valid, to_logit, zero)
        + pltpu.roll(jnp.where(valid, to_scale, zero), mixes, 1)
        + pltpu.roll(jnp.where(valid, to_shape, zero), 2 * mixes, 1)
    )
    return nll, grad


def backward_kernel(
    blocks,
    chunk,
    limit_hbm,
    pool_ref,
    act_hbm,
    slope_ref,
    skipw_hbm,
    tap_ref,
    res_ref,
    head1_ref,
    headb1_ref,
    head2_ref,
    headb2_ref,
    nll_ref,
    grad_ref,
    limit_ref,
    act_ref,
    skipw_ref,
    pad_ref,
    bias2_ref,
    sems,
):
    layers = tap_ref.shape[0]
    width = slope_ref.shape[1]
    limit_copy = pltpu.make_async_copy(limit_hbm, limit_ref, sems.at[0])
    copies = [
        pltpu.make_async_copy(skipw_hbm, skipw_ref, sems.at[1]),
        pltpu.make_async_copy(act_hbm, act_ref, sems.at[2]),
    ]
    limit_copy.start()
    start_all(copies)
    part = width // 2
    rows = blocks * chunk
    lanes = pad_ref.shape[0]
    outs = head2_ref.shape[0]
    base, chan_at, block_at, shard_base = position(blocks, chunk, 2)
    half = blocks // 2
    received = pool_ref[...].astype(F32)
    first = FIRST
    received = jnp.concatenate([received[blocks - first :], received[: blocks - first]], axis=0)
    sums = jnp.concatenate(
        [
            received[:half, :blocks, :].sum(axis=0),
            received[half:, :blocks, :].sum(axis=0),
        ],
        axis=0,
    )
    bins = jnp.concatenate([received[:, blocks, :lanes], received[:, blocks + 1, :lanes]], axis=0)
    seen = (
        jnp.concatenate(
            [received[:, blocks + 2, :lanes], received[:, blocks + 3, :lanes]], axis=0
        )
        == 1.0
    )
    log_time = jnp.log((bins + 1.0) / 8.0)
    window = lax.broadcasted_iota(jnp.int32, (2 * blocks, width), 0)
    start = (
        (window % blocks) * FIRST_DILATION
        + shard_base
        + (2 * chan_at + window // blocks) * WLEN
    )
    limit_copy.wait()
    limit = limit_ref[0]
    count = jnp.clip(limit - start, 1, WLEN).astype(F32)
    pooled = sums / count
    pad_ref[...] = jnp.zeros_like(pad_ref)
    pad_ref[:outs, :] = head2_ref[...]
    head1 = split(head1_ref[...])
    head2 = split(pad_ref[...])
    bias2_ref[...] = jnp.zeros_like(bias2_ref)
    bias2_ref[:, :outs] = headb2_ref[...]
    inner = fine_dot(pooled, head1, dot) + headb1_ref[...]
    open_inner = sigmoid(inner)
    hidden = inner * open_inner
    params = fine_dot(hidden, head2, dot_t) + bias2_ref[...]
    nll, to_params = mixture(params, log_time, seen, outs // 3)
    to_hidden = fine_dot(to_params, head2, dot)
    to_inner = to_hidden * open_inner * (1.0 + inner * (1.0 - open_inner))
    to_pooled = fine_dot(to_inner, head1, dot_t)

    row = lax.broadcasted_iota(jnp.int32, (2 * blocks, 2), 0)
    col = lax.broadcasted_iota(jnp.int32, (2 * blocks, 2), 1)
    mine = row == col * blocks + block_at
    nll_ref[...] = jnp.sum(jnp.where(mine, nll, 0.0), axis=0, keepdims=True)

    own_pool = jnp.where(block_at < half, to_pooled[:blocks], to_pooled[blocks:])
    spread = jnp.broadcast_to(own_pool[:, None, :], (blocks, chunk, width)).reshape(rows, width)
    wait_all(copies)
    grad_skip = (spread * slope_ref[...].astype(F32)).astype(BF16)
    grad_rows = None
    for layer in range(layers - 1, -1, -1):
        early = chunk * 2**layer
        grad_gated = dot_t(grad_skip, skipw_ref[layer])
        if grad_rows is not None:
            grad_gated = grad_gated + dot_t(grad_rows, res_ref[layer])
        twice = jnp.concatenate([grad_gated, grad_gated], axis=1)
        preact_grad = (twice * act_ref[layer].astype(F32)).astype(BF16)
        ahead = jnp.concatenate(
            [preact_grad[early:], jnp.zeros((early, 2 * width), BF16)], axis=0
        )
        summed = dot_t(preact_grad, tap_ref[layer, 1]) + dot_t(ahead, tap_ref[layer, 0])
        if grad_rows is not None:
            summed = summed + grad_rows.astype(F32)
        grad_rows = summed.astype(BF16)
    for c in range(2):
        for block, at, count in spans(blocks):
            piece = grad_rows[block * chunk : (block + count) * chunk, c * part : (c + 1) * part]
            grad_ref[at : at + count, 1 - c] = piece.reshape(count, chunk, part)


def local(
    signal,
    skip_in,
    tap_weight,
    tap_bias,
    res_weight,
    skip_weight,
    head_w1,
    head_b1,
    head_w2,
    head_second_bias,
    event_bin,
    observed,
    valid_len,
):
    blocks = lax.axis_size("blk")
    chans = lax.axis_size("chan")
    shard_rows, part = signal.shape
    width = part * chans
    peers = blocks * chans
    chunk = shard_rows // peers
    rows = blocks * chunk
    layers = tap_weight.shape[0]
    shape = jax.ShapeDtypeStruct
    smem = pl.BlockSpec(memory_space=pltpu.SMEM)
    vmem = pl.BlockSpec(memory_space=pltpu.VMEM)
    hbm = pl.BlockSpec(memory_space=pltpu.HBM)
    params = pltpu.CompilerParams(vmem_limit_bytes=24 << 20)

    def stay(array):
        return pltpu.with_memory_space_constraint(array, pltpu.HBM)


    both, limit = pl.pallas_call(
        join_kernel,
        out_shape=(shape((blocks, chans, 2, chunk, part), BF16), pltpu.HBM((8,), jnp.int32)),
        in_specs=[smem, hbm, hbm],
        out_specs=(vmem, hbm),
        scratch_shapes=[pltpu.SMEM((8,), jnp.int32), pltpu.SemaphoreType.DMA((9,))],
        compiler_params=params,
        cost_estimate=pl.CostEstimate(
            flops=40_000_000_000, bytes_accessed=2 * peers * chunk * part * 4, transcendentals=0
        ),
        name="join",
    )(valid_len, stay(signal.reshape(peers, chunk, part)), stay(skip_in.reshape(peers, chunk, part)))
    shards = lax.axis_size("j")
    everyone = ("blk", "j", "chan")
    order = [
        (chans - 1 - i % chans) * blocks + (FIRST + i // chans) % blocks for i in range(peers)
    ]
    wide = [
        [((k % blocks) * shards + j) * chans + k // blocks for k in order] for j in range(shards)
    ]
    first = FIRST
    near = [[(first + i) % blocks for i in range(blocks)]]
    both = both.reshape(peers, 2, chunk, part)
    both = lax.all_to_all(both, everyone, 0, 0, tiled=True, axis_index_groups=wide)
    both = both.reshape(blocks, chans, 2, chunk, part)

    acts, slope, pool = pl.pallas_call(
        lambda *refs: forward_kernel(blocks, chunk, *refs),
        out_shape=(
            pltpu.HBM((layers, rows, 2 * width), BF16),
            shape((rows, width), BF16),
            shape((blocks, blocks + 8, width), BF16),
        ),
        in_specs=[hbm] * 3 + [vmem] * 4 + [hbm],
        out_specs=(hbm, vmem, vmem),
        scratch_shapes=[
            pltpu.SMEM((8,), jnp.int32),
            pltpu.SMEM(event_bin.shape, jnp.int32),
            pltpu.SMEM(observed.shape, jnp.int32),
            pltpu.VMEM(skip_weight.shape, BF16),
            pltpu.VMEM((layers, rows, 2 * width), BF16),
            pltpu.SemaphoreType.DMA((4,)),
            pltpu.SemaphoreType.DMA((layers,)),
        ],
        compiler_params=params,
        cost_estimate=pl.CostEstimate(
            flops=40_000_000_000, bytes_accessed=8 << 20, transcendentals=0
        ),
        name="forward",
    )(
        stay(limit),
        stay(event_bin),
        stay(observed),
        both,
        tap_weight,
        tap_bias,
        res_weight,
        stay(skip_weight),
    )

    pool = lax.all_to_all(pool, "blk", 0, 0, tiled=True, axis_index_groups=near)

    head_b1 = head_b1.reshape(1, -1)
    head_second_bias = head_second_bias.reshape(1, -1)
    nll, grads = pl.pallas_call(
        lambda *refs: backward_kernel(blocks, chunk, *refs),
        out_shape=(
            shape((1, 2), F32),
            shape((blocks, chans, chunk, part), BF16),
        ),
        in_specs=[hbm, vmem, hbm, vmem, hbm] + [vmem] * 6,
        out_specs=(vmem, vmem),
        scratch_shapes=[
            pltpu.SMEM((8,), jnp.int32),
            pltpu.VMEM((layers, rows, 2 * width), BF16),
            pltpu.VMEM(skip_weight.shape, BF16),
            pltpu.VMEM((128, width), F32),
            pltpu.VMEM((1, 128), F32),
            pltpu.SemaphoreType.DMA((3,)),
        ],
        compiler_params=params,
        name="backward",
    )(
        stay(limit),
        pool,
        stay(acts),
        slope,
        stay(skip_weight),
        tap_weight,
        res_weight,
        head_w1,
        head_b1,
        head_w2.T,
        head_second_bias,
    )
    grads = grads.reshape(peers, chunk, part)
    grads = lax.all_to_all(grads, everyone, 0, 0, tiled=True, axis_index_groups=wide)
    grads = grads.reshape(blocks, chans, chunk, part)
    grads = pl.pallas_call(
        place_kernel,
        out_shape=pltpu.HBM((peers, chunk, part), BF16),
        in_specs=[vmem],
        out_specs=hbm,
        scratch_shapes=[pltpu.SemaphoreType.DMA((4,))],
        compiler_params=params,
        name="place",
    )(grads)
    return (nll.reshape(2), grads.reshape(shard_rows, part))


def solution(mesh):
    blocks = 16
    devices = mesh.devices
    split = Mesh(
        devices.reshape(blocks, devices.shape[0] // blocks, devices.shape[1]),
        ("blk", "j", "chan"),
    )
    time = ("blk", "j")
    return jax.shard_map(
        local,
        mesh=split,
        in_specs=(
            P(time, "chan"),
            P(time, "chan"),
            P(),
            P(),
            P(),
            P(),
            P(),
            P(),
            P(),
            P(),
            P(time),
            P(time),
            P(),
        ),
        out_specs=(P(("blk", "j", "chan")), P(time, "chan")),
        check_vma=False,
    )
```

```python
import jax
import jax.numpy as jnp
from jax import lax
from jax.experimental import pallas as pl
from jax.experimental.pallas import tpu as pltpu
from jax.sharding import Mesh
from jax.sharding import PartitionSpec as P

WLEN = 128
FIRST_DILATION = 8192
F32 = jnp.float32
BF16 = jnp.bfloat16
FIRST = 10


def dot(a, b):
    return jnp.dot(a, b, preferred_element_type=F32)


def dot_t(a, b):
    return lax.dot_general(a, b, (((1,), (1,)), ((), ())), preferred_element_type=F32)


def split(v):
    high = v.astype(BF16)
    return high, (v - high.astype(F32)).astype(BF16)


def fine_dot(a, b, product):
    high, low = split(a)
    rows = a.shape[0]
    both = product(jnp.concatenate([high, low], axis=0), b[0])
    return both[:rows] + both[rows:] + product(high, b[1])


def sigmoid(v):
    return 0.5 * jnp.tanh(0.5 * v) + 0.5


def position(blocks, chunk, chans):
    chan_at = lax.axis_index("chan")
    block_at = lax.axis_index("blk")
    shard_base = lax.axis_index("j") * (blocks * chans * chunk)
    base = shard_base + (chan_at * blocks + block_at) * chunk
    return base, chan_at, block_at, shard_base


def row_keep(limit, base, blocks, chunk, width):
    shape = (blocks, chunk, width)
    block = lax.broadcasted_iota(jnp.int32, shape, 0)
    offset = lax.broadcasted_iota(jnp.int32, shape, 1)
    position = (block * FIRST_DILATION + offset + base).reshape(blocks * chunk, width)
    return position < limit


def start_all(copies):
    for copy in copies:
        copy.start()


def wait_all(copies):
    for copy in copies:
        copy.wait()


def spans(blocks):
    lead = blocks - FIRST
    return [(FIRST, 0, lead), (0, lead, FIRST)]


def join_kernel(limit_ref, signal_ref, skip_ref, both_ref, limit_hbm, hold_ref, sems):
    hold_ref[0] = limit_ref[0]
    copies = [pltpu.make_async_copy(hold_ref, limit_hbm, sems.at[0])]
    blocks, chans = both_ref.shape[:2]
    for c in range(chans):
        for block, at, count in spans(blocks):
            for part, ref in enumerate((signal_ref, skip_ref)):
                copies.append(
                    pltpu.make_async_copy(
                        ref.at[pl.ds(c * blocks + block, count)],
                        both_ref.at[pl.ds(at, count), chans - 1 - c, part],
                        sems.at[len(copies)],
                    )
                )
    start_all(copies)
    wait_all(copies)


def place_kernel(received_ref, grad_hbm, sems):
    copies = []
    blocks, chans = received_ref.shape[:2]
    for c in range(chans):
        for block, at, count in spans(blocks):
            copies.append(
                pltpu.make_async_copy(
                    received_ref.at[pl.ds(at, count), chans - 1 - c],
                    grad_hbm.at[pl.ds(c * blocks + block, count)],
                    sems.at[len(copies)],
                )
            )
    start_all(copies)
    wait_all(copies)


def read_turned(ref, c, part):
    blocks, chans = ref.shape[:2]
    pieces = [
        ref[at : at + count, chans - 1 - c, part].reshape(count * ref.shape[3], ref.shape[4])
        for _, at, count in sorted(spans(blocks))
    ]
    return jnp.concatenate(pieces, axis=0)


def forward_kernel(
    blocks,
    chunk,
    limit_hbm,
    bin_hbm,
    seen_hbm,
    both_ref,
    tap_ref,
    bias_ref,
    res_ref,
    skipw_hbm,
    act_hbm,
    slope_ref,
    pool_ref,
    limit_ref,
    bin_ref,
    seen_ref,
    skipw_ref,
    act_ref,
    in_sems,
    out_sems,
):
    layers = tap_ref.shape[0]
    part = both_ref.shape[4]
    width = 2 * part
    rows = blocks * chunk
    base, chan_at, _, _ = position(blocks, chunk, 2)
    scalars = [
        pltpu.make_async_copy(limit_hbm, limit_ref, in_sems.at[0]),
        pltpu.make_async_copy(bin_hbm, bin_ref, in_sems.at[1]),
        pltpu.make_async_copy(seen_hbm, seen_ref, in_sems.at[2]),
    ]
    skipw_copy = pltpu.make_async_copy(skipw_hbm, skipw_ref, in_sems.at[3])
    skipw_copy.start()
    start_all(scalars)
    outs = []
    gated_all = []
    current, skip_sum = (
        jnp.concatenate(
            [read_turned(both_ref, c, part_at) for c in range(2)], axis=1
        )
        for part_at in range(2)
    )
    skip_sum = skip_sum.astype(F32)
    for layer in range(layers):
        late = chunk * 2**layer
        delayed = jnp.concatenate(
            [jnp.zeros((late, width), BF16), current[: rows - late]], axis=0
        )
        preact = (
            dot(delayed, tap_ref[layer, 0])
            + dot(current, tap_ref[layer, 1])
            + bias_ref[layer : layer + 1, :]
        )
        filters = jnp.tanh(preact[:, :width])
        gates = sigmoid(preact[:, width:])
        product = filters * gates
        gated = product.astype(BF16)
        gated_all.append(gated)
        if layer < layers - 1:
            current = (current.astype(F32) + dot(gated, res_ref[layer])).astype(BF16)
        act_ref[layer, :, :width] = (gates - product * filters).astype(BF16)
        act_ref[layer, :, width:] = (product - product * gates).astype(BF16)
        outs.append(
            pltpu.make_async_copy(act_ref.at[layer], act_hbm.at[layer], out_sems.at[layer])
        )
        outs[-1].start()
        if layer == 1:
            skipw_copy.wait()
        if layer > 0:
            skip_sum = skip_sum + dot(gated_all[layer - 1], skipw_ref[layer - 1])
    skip_sum = skip_sum + dot(gated_all[layers - 1], skipw_ref[layers - 1])
    wait_all(scalars)
    limit = limit_ref[0]
    keep = row_keep(limit, base, blocks, chunk, width)
    sig = sigmoid(skip_sum)
    slope = sig * (1.0 + skip_sum * (1.0 - sig))
    slope_ref[...] = jnp.where(keep, slope, 0.0).astype(BF16)
    active = jnp.where(keep, skip_sum * sig, 0.0)
    sums = active.reshape(blocks, chunk, width).sum(axis=1)
    first = 2 * chan_at
    line = lax.broadcasted_iota(jnp.int32, (8, width), 0)
    bins = [ref[first + i].astype(F32) for ref in (bin_ref, seen_ref) for i in (0, 1)]
    extra = jnp.where(
        line == 0,
        bins[0],
        jnp.where(line == 1, bins[1], jnp.where(line == 2, bins[2], bins[3])),
    )
    sums = sums.astype(BF16)
    extra = extra.astype(BF16)
    for other in range(blocks):
        pool_ref[other, :blocks, :] = sums
        pool_ref[other, blocks:, :] = extra
    wait_all(outs)


def mixture(params, log_time, seen, mixes):
    lanes = params.shape[1]
    lane = lax.broadcasted_iota(jnp.int32, params.shape, 1)
    valid = lane < mixes
    bend_logit = jnp.tanh(params)
    log_scale = jnp.tanh(pltpu.roll(params, lanes - mixes, 1))
    bend_shape = jnp.tanh(pltpu.roll(params, lanes - 2 * mixes, 1))
    logits = 4.0 * bend_logit
    raised = jnp.where(valid, jnp.exp(logits), 0.0)
    total = jnp.sum(raised, axis=1, keepdims=True)
    log_weight = logits - jnp.log(total)
    log_shape = 0.5 * bend_shape
    shape = jnp.exp(log_shape)
    ratio = log_time - log_scale
    power = jnp.exp(shape * ratio)
    density = log_shape - log_scale + (shape - 1.0) * ratio - power
    component = jnp.where(seen, density, -power)
    likely = jnp.where(valid, jnp.exp(log_weight + component), 0.0)
    mass = jnp.sum(likely, axis=1, keepdims=True)
    nll = -jnp.log(mass)
    owned = likely / mass
    to_logit = (raised / total - owned) * 4.0 * (1.0 - bend_logit * bend_logit)
    steep = power * shape
    to_scale = jnp.where(seen, steep - shape, steep)
    to_shape = jnp.where(seen, 1.0 + shape * ratio, 0.0) - steep * ratio
    to_scale = -owned * to_scale * (1.0 - log_scale * log_scale)
    to_shape = -owned * to_shape * 0.5 * (1.0 - bend_shape * bend_shape)
    zero = jnp.zeros_like(params)
    grad = (
        jnp.where(valid, to_logit, zero)
        + pltpu.roll(jnp.where(valid, to_scale, zero), mixes, 1)
        + pltpu.roll(jnp.where(valid, to_shape, zero), 2 * mixes, 1)
    )
    return nll, grad


def backward_kernel(
    blocks,
    chunk,
    limit_hbm,
    pool_ref,
    act_hbm,
    slope_ref,
    skipw_hbm,
    tap_ref,
    res_ref,
    head1_ref,
    headb1_ref,
    head2_ref,
    headb2_ref,
    nll_ref,
    grad_ref,
    limit_ref,
    act_ref,
    skipw_ref,
    pad_ref,
    bias2_ref,
    sems,
):
    layers = tap_ref.shape[0]
    width = slope_ref.shape[1]
    limit_copy = pltpu.make_async_copy(limit_hbm, limit_ref, sems.at[0])
    copies = [
        pltpu.make_async_copy(skipw_hbm, skipw_ref, sems.at[1]),
        pltpu.make_async_copy(act_hbm, act_ref, sems.at[2]),
    ]
    limit_copy.start()
    start_all(copies)
    part = width // 2
    rows = blocks * chunk
    lanes = pad_ref.shape[0]
    outs = head2_ref.shape[0]
    base, chan_at, block_at, shard_base = position(blocks, chunk, 2)
    half = blocks // 2
    received = pool_ref[...].astype(F32)
    first = FIRST
    received = jnp.concatenate([received[blocks - first :], received[: blocks - first]], axis=0)
    sums = jnp.concatenate(
        [
            received[:half, :blocks, :].sum(axis=0),
            received[half:, :blocks, :].sum(axis=0),
        ],
        axis=0,
    )
    bins = jnp.concatenate([received[:, blocks, :lanes], received[:, blocks + 1, :lanes]], axis=0)
    seen = (
        jnp.concatenate(
            [received[:, blocks + 2, :lanes], received[:, blocks + 3, :lanes]], axis=0
        )
        == 1.0
    )
    log_time = jnp.log((bins + 1.0) / 8.0)
    start = lax.broadcasted_iota(jnp.int32, (blocks, width), 0) * FIRST_DILATION
    limit_copy.wait()
    left = limit_ref[0] - shard_base - 2 * chan_at * WLEN
    left = jnp.concatenate([left - start, left - WLEN - start], axis=0)
    count = jnp.clip(left, 1, WLEN).astype(F32)
    pooled = sums / count
    pad_ref[...] = jnp.zeros_like(pad_ref)
    pad_ref[:outs, :] = head2_ref[...]
    head1 = split(head1_ref[...])
    head2 = split(pad_ref[...])
    bias2_ref[...] = jnp.zeros_like(bias2_ref)
    bias2_ref[:, :outs] = headb2_ref[...]
    inner = fine_dot(pooled, head1, dot) + headb1_ref[...]
    open_inner = sigmoid(inner)
    hidden = inner * open_inner
    params = fine_dot(hidden, head2, dot_t) + bias2_ref[...]
    nll, to_params = mixture(params, log_time, seen, outs // 3)
    to_hidden = fine_dot(to_params, head2, dot)
    to_inner = to_hidden * open_inner * (1.0 + inner * (1.0 - open_inner))
    to_pooled = fine_dot(to_inner, head1, dot_t)

    row = lax.broadcasted_iota(jnp.int32, (2 * blocks, 2), 0)
    col = lax.broadcasted_iota(jnp.int32, (2 * blocks, 2), 1)
    mine = row == col * blocks + block_at
    nll_ref[...] = jnp.sum(jnp.where(mine, nll, 0.0), axis=0, keepdims=True)

    own_pool = jnp.where(block_at < half, to_pooled[:blocks], to_pooled[blocks:])
    spread = jnp.broadcast_to(own_pool[:, None, :], (blocks, chunk, width)).reshape(rows, width)
    wait_all(copies)
    grad_skip = (spread * slope_ref[...].astype(F32)).astype(BF16)
    grad_rows = None
    for layer in range(layers - 1, -1, -1):
        early = chunk * 2**layer
        grad_gated = dot_t(grad_skip, skipw_ref[layer])
        if grad_rows is not None:
            grad_gated = grad_gated + dot_t(grad_rows, res_ref[layer])
        twice = jnp.concatenate([grad_gated, grad_gated], axis=1)
        preact_grad = (twice * act_ref[layer].astype(F32)).astype(BF16)
        ahead = jnp.concatenate(
            [preact_grad[early:], jnp.zeros((early, 2 * width), BF16)], axis=0
        )
        summed = dot_t(preact_grad, tap_ref[layer, 1]) + dot_t(ahead, tap_ref[layer, 0])
        if grad_rows is not None:
            summed = summed + grad_rows.astype(F32)
        grad_rows = summed.astype(BF16)
    for c in range(2):
        for block, at, count in spans(blocks):
            piece = grad_rows[block * chunk : (block + count) * chunk, c * part : (c + 1) * part]
            grad_ref[at : at + count, 1 - c] = piece.reshape(count, chunk, part)


def local(
    signal,
    skip_in,
    tap_weight,
    tap_bias,
    res_weight,
    skip_weight,
    head_w1,
    head_b1,
    head_w2,
    head_second_bias,
    event_bin,
    observed,
    valid_len,
):
    blocks = lax.axis_size("blk")
    chans = lax.axis_size("chan")
    shard_rows, part = signal.shape
    width = part * chans
    peers = blocks * chans
    chunk = shard_rows // peers
    rows = blocks * chunk
    layers = tap_weight.shape[0]
    shape = jax.ShapeDtypeStruct
    smem = pl.BlockSpec(memory_space=pltpu.SMEM)
    vmem = pl.BlockSpec(memory_space=pltpu.VMEM)
    hbm = pl.BlockSpec(memory_space=pltpu.HBM)
    params = pltpu.CompilerParams(vmem_limit_bytes=24 << 20)

    def stay(array):
        return pltpu.with_memory_space_constraint(array, pltpu.HBM)


    both, limit = pl.pallas_call(
        join_kernel,
        out_shape=(shape((blocks, chans, 2, chunk, part), BF16), pltpu.HBM((8,), jnp.int32)),
        in_specs=[smem, hbm, hbm],
        out_specs=(vmem, hbm),
        scratch_shapes=[pltpu.SMEM((8,), jnp.int32), pltpu.SemaphoreType.DMA((9,))],
        compiler_params=params,
        cost_estimate=pl.CostEstimate(
            flops=40_000_000_000, bytes_accessed=2 * peers * chunk * part * 4, transcendentals=0
        ),
        name="join",
    )(valid_len, stay(signal.reshape(peers, chunk, part)), stay(skip_in.reshape(peers, chunk, part)))
    shards = lax.axis_size("j")
    everyone = ("blk", "j", "chan")
    order = [
        (chans - 1 - i % chans) * blocks + (FIRST + i // chans) % blocks for i in range(peers)
    ]
    wide = [
        [((k % blocks) * shards + j) * chans + k // blocks for k in order] for j in range(shards)
    ]
    first = FIRST
    near = [[(first + i) % blocks for i in range(blocks)]]
    both = both.reshape(peers, 2, chunk, part)
    both = lax.all_to_all(both, everyone, 0, 0, tiled=True, axis_index_groups=wide)
    both = both.reshape(blocks, chans, 2, chunk, part)

    acts, slope, pool = pl.pallas_call(
        lambda *refs: forward_kernel(blocks, chunk, *refs),
        out_shape=(
            pltpu.HBM((layers, rows, 2 * width), BF16),
            shape((rows, width), BF16),
            shape((blocks, blocks + 8, width), BF16),
        ),
        in_specs=[hbm] * 3 + [vmem] * 4 + [hbm],
        out_specs=(hbm, vmem, vmem),
        scratch_shapes=[
            pltpu.SMEM((8,), jnp.int32),
            pltpu.SMEM(event_bin.shape, jnp.int32),
            pltpu.SMEM(observed.shape, jnp.int32),
            pltpu.VMEM(skip_weight.shape, BF16),
            pltpu.VMEM((layers, rows, 2 * width), BF16),
            pltpu.SemaphoreType.DMA((4,)),
            pltpu.SemaphoreType.DMA((layers,)),
        ],
        compiler_params=params,
        cost_estimate=pl.CostEstimate(
            flops=40_000_000_000, bytes_accessed=8 << 20, transcendentals=0
        ),
        name="forward",
    )(
        stay(limit),
        stay(event_bin),
        stay(observed),
        both,
        tap_weight,
        tap_bias,
        res_weight,
        stay(skip_weight),
    )

    pool = lax.all_to_all(pool, "blk", 0, 0, tiled=True, axis_index_groups=near)

    head_b1 = head_b1.reshape(1, -1)
    head_second_bias = head_second_bias.reshape(1, -1)
    nll, grads = pl.pallas_call(
        lambda *refs: backward_kernel(blocks, chunk, *refs),
        out_shape=(
            shape((1, 2), F32),
            shape((blocks, chans, chunk, part), BF16),
        ),
        in_specs=[hbm, vmem, hbm, vmem, hbm] + [vmem] * 6,
        out_specs=(vmem, vmem),
        scratch_shapes=[
            pltpu.SMEM((8,), jnp.int32),
            pltpu.VMEM((layers, rows, 2 * width), BF16),
            pltpu.VMEM(skip_weight.shape, BF16),
            pltpu.VMEM((128, width), F32),
            pltpu.VMEM((1, 128), F32),
            pltpu.SemaphoreType.DMA((3,)),
        ],
        compiler_params=params,
        name="backward",
    )(
        stay(limit),
        pool,
        stay(acts),
        slope,
        stay(skip_weight),
        tap_weight,
        res_weight,
        head_w1,
        head_b1,
        head_w2.T,
        head_second_bias,
    )
    grads = grads.reshape(peers, chunk, part)
    grads = lax.all_to_all(grads, everyone, 0, 0, tiled=True, axis_index_groups=wide)
    grads = grads.reshape(blocks, chans, chunk, part)
    grads = pl.pallas_call(
        place_kernel,
        out_shape=pltpu.HBM((peers, chunk, part), BF16),
        in_specs=[vmem],
        out_specs=hbm,
        scratch_shapes=[pltpu.SemaphoreType.DMA((4,))],
        compiler_params=params,
        name="place",
    )(grads)
    return (nll.reshape(2), grads.reshape(shard_rows, part))


def solution(mesh):
    blocks = 16
    devices = mesh.devices
    split = Mesh(
        devices.reshape(blocks, devices.shape[0] // blocks, devices.shape[1]),
        ("blk", "j", "chan"),
    )
    time = ("blk", "j")
    return jax.shard_map(
        local,
        mesh=split,
        in_specs=(
            P(time, "chan"),
            P(time, "chan"),
            P(),
            P(),
            P(),
            P(),
            P(),
            P(),
            P(),
            P(),
            P(time),
            P(time),
            P(),
        ),
        out_specs=(P(("blk", "j", "chan")), P(time, "chan")),
        check_vma=False,
    )
```
